32 devices in a mesh: graph: 8 (over z, y), mp: 4 (over x, core).
Axes of the slice: x: 2, y: 2, z: 4, core: 2. Of those that a mesh axis runs over, the one named last changes fastest.
Arguments:
- node_features: bfloat16 [16, 128, 1024], P('graph'), may hold values from -24 to 24
- wq: bfloat16 [1024, 4, 256], P(None, 'mp'), may hold values from -0.375 to 0.375
- wkv: bfloat16 [1024, 4, 128], P(None, 'mp'), may hold values from -0.1875 to 0.1875
- wo: bfloat16 [4, 256, 1024], P('mp'), may hold values from -0.1875 to 0.1875
- send_list: int32 [8, 8, 1], P('graph'), may hold values from 0 to 1
- block_list: int32 [16, 32], P('graph'), may hold values from 0 to 7, as said below
- cotangent: bfloat16 [2048, 1024], P('graph'), may hold values from -0.75 to 0.75
Outputs:
- layer_output: bfloat16 [2048, 1024], P(('graph', 'mp'))
- grad_wq: float32 [1024, 4, 256], P('graph', 'mp')
- grad_wkv: float32 [1024, 4, 128], P('graph', 'mp')
- grad_wo: float32 [4, 256, 1024], P('mp', None, 'graph')
The draws below stay inside these ranges and needn't reach their ends.
Inputs may be any that keep to these rules, and one draw needn't show every extreme that they name: `send_list`: each entry is a tile index local to the sending partition. `block_list`: entry b names slot b % 1 filled by partition b // 1 for the query tile's partition. The entries of one partition's tiles, read row by row, run through a random order of all 8 slot numbers and then start that order again.
All inputs are finite; a program needn't handle non-finite values.
Results may differ from the reference program's by a relative error of at most 0.0035.
The reference program's roundings to bfloat16 on the way count: a program that leaves them out, or rounds other values in their place, can miss the bound.
Values may be sent and summed in bfloat16 or wider, within the bound.
No kernel may reach another device: no remote copies, remote signals or barrier semaphores. Data moves between devices by JAX's collectives and lax.ppermute only.
A program may use at most 64 MiB of HBM per device.

```python
import jax
import jax.numpy as jnp
from jax import lax

D = 1024
KVH = 4
GQ = 4
DH = 64
TILE = 128
NB = 32
SLOTS = 1
TILE_DEV = 2
TILES = 16
TOKENS = 2048
N_GRAPH = 8


def draw_node_features(key, part):
    base = jnp.clip(jax.random.normal(key, (TILES, TILE, D), jnp.float32), -6.0, 6.0)
    return base.astype(jnp.bfloat16)


def draw_block_list(key, part):
    count = N_GRAPH * SLOTS
    keys = jax.random.split(jax.random.fold_in(key, 11), N_GRAPH)
    orders = jax.vmap(lambda one: jax.random.permutation(one, count))(keys)
    picks = jnp.arange(TILE_DEV * NB, dtype=jnp.int32) % count
    return orders[:, picks].reshape(TILES, NB).astype(jnp.int32)


def set_ends(array, rng, low, largest):
    index_at = [jax.random.randint(jax.random.fold_in(rng, axis), (), 0, length) for axis, length in enumerate(array.shape)]
    longest = array.shape.index(max(array.shape))
    neighbour = index_at[:longest] + [(index_at[longest] + 1) % array.shape[longest]] + index_at[longest + 1:]
    return array.at[tuple(index_at)].set(low).at[tuple(neighbour)].set(largest)


def steps_of(own_key, extent, shards, low, largest):
    factor_of, own = 1.0, jax.random.fold_in(own_key, 6)
    for dim, blocks in shards:
        heights = jnp.exp(jax.random.uniform(jax.random.fold_in(own, dim), (blocks,), jnp.float32, low / len(shards), largest / len(shards)))
        factor_of = factor_of * jnp.repeat(heights, extent[dim] // blocks).reshape([-1 if axis == dim else 1 for axis in range(len(extent))])
    return factor_of


def bell_draw(stream_key, extent, deviation, reach, pieces=(), kind=jnp.bfloat16):
    values = jax.random.normal(stream_key, extent, jnp.float32) * deviation
    if len(pieces) > 0:
        values = steps_of(stream_key, extent, pieces, -0.22, 0.18) * values
    return jnp.clip(values, min=-reach, max=reach).astype(kind)


def setup_inputs(seed: int = 0) -> dict:
    seeds = jax.random.split(jax.random.key(seed), 8)
    node_features = draw_node_features(jax.random.fold_in(seeds[7], 71), 0)
    wq = bell_draw(seeds[1], (D, KVH, GQ * DH), (D // 4) ** -0.5, 0.375, ((1, 4),))
    wkv = bell_draw(seeds[2], (D, KVH, 2 * DH), D ** -0.5, 0.1875, ((1, 4),))
    wo = bell_draw(seeds[3], (KVH, GQ * DH, D), D ** -0.5, 0.1875, ((0, 4),))
    send_list = set_ends(jax.random.randint(seeds[4], (N_GRAPH, N_GRAPH, SLOTS), 0, TILE_DEV), jax.random.fold_in(seeds[4], 1), 0, TILE_DEV - 1).astype(jnp.int32)
    block_list = draw_block_list(jax.random.fold_in(seeds[7], 71), 0)
    cotangent = bell_draw(seeds[6], (TOKENS, D), 0.05, 0.75, ((0, 8),))
    return dict(node_features=node_features, wq=wq, wkv=wkv, wo=wo, send_list=send_list, block_list=block_list, cotangent=cotangent)


def forward_tile(query_tile, key_rows):
    key_flat = key_rows.reshape(-1, KVH, 2 * DH).astype(jnp.float32)
    score = jnp.einsum("rhgd,khd->hgrk", query_tile.astype(jnp.float32), key_flat[..., :DH])
    row_max = jnp.max(score, axis=-1, keepdims=True)
    exponent = jnp.exp(score - row_max)
    weights = exponent / jnp.sum(exponent, axis=-1, keepdims=True)
    rounded = lax.optimization_barrier(weights.astype(jnp.bfloat16)).astype(jnp.float32)
    mixed = jnp.einsum("hgrk,khd->rhgd", rounded, key_flat[..., DH:]).astype(jnp.bfloat16)
    return weights, rounded, mixed


def backward_tile(query_tile, key_rows, grad_tile):
    weights, rounded, unused_mixed = forward_tile(query_tile, key_rows)
    key_flat = key_rows.reshape(-1, KVH, 2 * DH).astype(jnp.float32)
    grad_float = grad_tile.astype(jnp.float32)
    grad_prob = jnp.einsum("rhgd,khd->hgrk", grad_float, key_flat[..., DH:])
    delta = jnp.sum(weights * grad_prob, axis=-1, keepdims=True)
    grad_score = lax.optimization_barrier((weights * (grad_prob - delta)).astype(jnp.bfloat16)).astype(jnp.float32)
    grad_query = (jnp.einsum("hgrk,khd->rhgd", grad_score, key_flat[..., :DH]) * (DH ** -0.5)).astype(jnp.bfloat16)
    grad_key = jnp.einsum("hgrk,rhgd->khd", grad_score, query_tile.astype(jnp.float32))
    grad_value = jnp.einsum("hgrk,rhgd->khd", rounded, grad_float)
    key_grad = jnp.concatenate([grad_key, grad_value], axis=-1).reshape(key_rows.shape)
    return grad_query, key_grad


def reference(node_features, wq, wkv, wo, send_list, block_list, cotangent):
    token_rows = node_features.reshape(TOKENS, D)
    query = (jnp.dot(token_rows, wq.reshape(D, -1), preferred_element_type=jnp.float32) * (DH ** -0.5)).astype(jnp.bfloat16)
    query = query.reshape(TILES, TILE, KVH, GQ, DH)
    keyval = jnp.dot(token_rows, wkv.reshape(D, -1), preferred_element_type=jnp.float32).astype(jnp.bfloat16)
    keyval = keyval.reshape(TILES, TILE, KVH, 2 * DH)
    owner = jnp.arange(TILES, dtype=jnp.int32) // TILE_DEV
    source = block_list // SLOTS
    slot = block_list % SLOTS
    key_tile = (source * TILE_DEV + send_list[source, owner[:, None], slot]).astype(jnp.int32)

    def forward_one(entry):
        query_tile, key_ids = entry
        return forward_tile(query_tile, keyval[key_ids])[2]

    mixed = lax.map(forward_one, (query, key_tile))
    mixed_rows = mixed.reshape(TOKENS, D)
    out_flat = wo.reshape(D, D)
    layer_output = (token_rows.astype(jnp.float32) + jnp.dot(mixed_rows, out_flat, preferred_element_type=jnp.float32)).astype(jnp.bfloat16)

    grad_rows = cotangent.reshape(TOKENS, D)
    grad_wo = jnp.dot(mixed_rows.T, grad_rows, preferred_element_type=jnp.float32).reshape(KVH, GQ * DH, D)
    grad_mixed = jnp.dot(grad_rows, out_flat.T, preferred_element_type=jnp.float32).astype(jnp.bfloat16)
    grad_mixed = grad_mixed.reshape(TILES, TILE, KVH, GQ, DH)

    slot_ids = jnp.arange(N_GRAPH * SLOTS, dtype=jnp.int32)
    slot_source = slot_ids // SLOTS
    slot_index = slot_ids % SLOTS

    def per_part(accum, part_index):
        start = part_index * TILE_DEV
        query_part = lax.dynamic_slice_in_dim(query, start, TILE_DEV, 0)
        ids_part = lax.dynamic_slice_in_dim(key_tile, start, TILE_DEV, 0)
        grad_part = lax.dynamic_slice_in_dim(grad_mixed, start, TILE_DEV, 0)
        blocks = lax.dynamic_slice_in_dim(block_list, start, TILE_DEV, 0)

        def backward_one(entry):
            query_tile, key_ids, grad_tile = entry
            return backward_tile(query_tile, keyval[key_ids], grad_tile)

        grad_query, key_grad = lax.map(backward_one, (query_part, ids_part, grad_part))
        picks = (blocks.reshape(1, -1) == slot_ids[:, None]).astype(jnp.float32)
        slot_grad = jnp.dot(picks, key_grad.reshape(TILE_DEV * NB, -1), precision=lax.Precision.HIGHEST).astype(jnp.bfloat16)
        slot_grad = slot_grad.reshape(N_GRAPH * SLOTS, TILE, KVH, 2 * DH)
        target = (slot_source * TILE_DEV + send_list[slot_source, part_index, slot_index]).astype(jnp.int32)
        accum = accum.at[target].add(slot_grad.astype(jnp.float32))
        return accum, grad_query

    start_accum = jnp.zeros((TILES, TILE, KVH, 2 * DH), jnp.float32)
    accum, grad_query = lax.scan(per_part, start_accum, jnp.arange(N_GRAPH, dtype=jnp.int32))
    grad_keyval = accum.astype(jnp.bfloat16).reshape(TOKENS, -1)
    grad_query = grad_query.reshape(TOKENS, D)
    grad_wq = jnp.dot(token_rows.T, grad_query, preferred_element_type=jnp.float32).reshape(D, KVH, GQ * DH)
    grad_wkv = jnp.dot(token_rows.T, grad_keyval, preferred_element_type=jnp.float32).reshape(D, KVH, 2 * DH)
    return (layer_output, grad_wq, grad_wkv, grad_wo)
```

```python
import functools

import jax
import jax.numpy as jnp
from jax import lax
from jax.experimental import pallas as pl
from jax.experimental.pallas import tpu as pltpu
from jax.sharding import PartitionSpec as P

DH = 64
F32 = jnp.float32
BF16 = jnp.bfloat16


def head_forward(query_head, key_flat, width):
    score = jnp.einsum(
        "rhd,khd->hrk", query_head, key_flat[..., :width], preferred_element_type=F32
    )
    row_max = jnp.max(score, axis=-1, keepdims=True)
    exponent = jnp.exp(score - row_max)
    weights = exponent / jnp.sum(exponent, axis=-1, keepdims=True)
    rounded = weights.astype(BF16)
    mixed = jnp.einsum(
        "hrk,khd->rhd", rounded, key_flat[..., width:], preferred_element_type=F32
    ).astype(BF16)
    return (weights, rounded, mixed)


def tile_forward(query_tile, key_rows):
    heads = query_tile.shape[1]
    width = query_tile.shape[3]
    key_flat = key_rows.reshape(-1, heads, 2 * width)

    def one_head(query_head):
        return head_forward(query_head, key_flat, width)[2]

    per_head = lax.map(one_head, jnp.moveaxis(query_tile, 2, 0))
    return jnp.moveaxis(per_head, 0, 2)


def tile_backward(query_tile, key_rows, grad_tile):
    heads = query_tile.shape[1]
    width = query_tile.shape[3]
    key_flat = key_rows.reshape(-1, heads, 2 * width)

    def one_head(total, entry):
        query_head, grad_head = entry
        weights, rounded, unused_mixed = head_forward(query_head, key_flat, width)
        grad_prob = jnp.einsum(
            "rhd,khd->hrk", grad_head, key_flat[..., width:], preferred_element_type=F32
        )
        delta = jnp.sum(weights * grad_prob, axis=-1, keepdims=True)
        grad_score = (weights * (grad_prob - delta)).astype(BF16)
        grad_query = (
            jnp.einsum(
                "hrk,khd->rhd", grad_score, key_flat[..., :width], preferred_element_type=F32
            )
            * width ** (-0.5)
        ).astype(BF16)
        grad_key = jnp.einsum("hrk,rhd->khd", grad_score, query_head, preferred_element_type=F32)
        grad_value = jnp.einsum("hrk,rhd->khd", rounded, grad_head, preferred_element_type=F32)
        total = total + jnp.concatenate([grad_key, grad_value], axis=-1)
        return (total, grad_query)

    start_total = jnp.zeros(key_flat.shape, F32)
    key_grad, grad_query = lax.scan(
        one_head, start_total, (jnp.moveaxis(query_tile, 2, 0), jnp.moveaxis(grad_tile, 2, 0))
    )
    return (jnp.moveaxis(grad_query, 0, 2), key_grad.reshape(key_rows.shape))


def listed_local(node_features, wq, wkv, wo, send_list, block_list, cotangent):
    tiles, tile_rows, width = node_features.shape
    heads = wq.shape[1]
    head_width = wq.shape[2]
    groups = head_width // DH
    parts = lax.axis_size("graph")
    slots = send_list.shape[2]
    token_rows = node_features.reshape(tiles * tile_rows, width)
    query = (
        jnp.dot(token_rows, wq.reshape(width, -1), preferred_element_type=F32) * DH ** (-0.5)
    ).astype(BF16)
    query = query.reshape(tiles, tile_rows, heads, groups, DH)
    keyval = jnp.dot(token_rows, wkv.reshape(width, -1), preferred_element_type=F32).astype(BF16)
    keyval = keyval.reshape(tiles, tile_rows, -1)
    outgoing = keyval[send_list[0].reshape(-1)]
    received = lax.all_to_all(outgoing, "graph", split_axis=0, concat_axis=0, tiled=True)

    def forward_one(entry):
        query_tile, key_ids = entry
        return tile_forward(query_tile, received[key_ids])

    mixed = lax.map(forward_one, (query, block_list))
    mixed_rows = mixed.reshape(tiles * tile_rows, heads * head_width)
    out_flat = wo.reshape(heads * head_width, width)
    share = tiles * tile_rows // lax.axis_size("mp")
    summed = lax.psum_scatter(
        jnp.dot(mixed_rows, out_flat, preferred_element_type=F32),
        "mp",
        scatter_dimension=0,
        tiled=True,
    )
    own_rows = lax.dynamic_slice_in_dim(token_rows, lax.axis_index("mp") * share, share, 0)
    output = (own_rows.astype(F32) + summed).astype(BF16)
    grad_out_local = jnp.dot(mixed_rows.T, cotangent, preferred_element_type=F32).reshape(wo.shape)
    grad_mixed = jnp.einsum("rd,hd->rh", cotangent, out_flat, preferred_element_type=F32).astype(
        BF16
    )
    grad_mixed = grad_mixed.reshape(tiles, tile_rows, heads, groups, DH)

    def backward_one(entry):
        query_tile, key_ids, grad_tile = entry
        return tile_backward(query_tile, received[key_ids], grad_tile)

    grad_query, key_grad = lax.map(backward_one, (query, block_list, grad_mixed))
    slot_ids = jnp.arange(parts * slots, dtype=jnp.int32)
    picks = (block_list.reshape(1, -1) == slot_ids[:, None]).astype(F32)
    slot_grad = jnp.dot(
        picks,
        key_grad.reshape(tiles * block_list.shape[1], -1),
        precision=lax.Precision.HIGHEST,
        preferred_element_type=F32,
    ).astype(BF16)
    slot_grad = slot_grad.reshape(parts * slots, tile_rows, -1)
    returned = lax.all_to_all(slot_grad, "graph", split_axis=0, concat_axis=0, tiled=True)
    owners = (send_list[0].reshape(1, -1) == jnp.arange(tiles, dtype=jnp.int32)[:, None]).astype(
        BF16
    )
    grad_keyval = jnp.dot(
        owners, returned.reshape(parts * slots, -1), preferred_element_type=F32
    ).astype(BF16)
    grad_keyval = grad_keyval.reshape(tiles * tile_rows, -1)
    grad_query_local = jnp.dot(
        token_rows.T, grad_query.reshape(tiles * tile_rows, -1), preferred_element_type=F32
    ).reshape(wq.shape)
    grad_keyval_local = jnp.dot(token_rows.T, grad_keyval, preferred_element_type=F32).reshape(
        wkv.shape
    )
    grad_wq = lax.psum_scatter(grad_query_local, "graph", scatter_dimension=0, tiled=True)
    grad_wkv = lax.psum_scatter(grad_keyval_local, "graph", scatter_dimension=0, tiled=True)
    grad_out = lax.psum_scatter(grad_out_local, "graph", scatter_dimension=2, tiled=True)
    return (output, grad_wq, grad_wkv, grad_out)


def dot(a, b, contract=((1,), (0,))):
    return lax.dot_general(a, b, (contract, ((), ())), preferred_element_type=F32)


NT = ((1,), (1,))


def keyval_kernel(send_ref, x_ref, wkv_ref, out_ref, kv_ref):
    rows = out_ref.shape[1]
    kv = dot(x_ref[...], wkv_ref[...]).astype(BF16)
    for t in range(kv_ref.shape[0]):
        kv_ref[t] = kv[t * rows : (t + 1) * rows]
    for r in range(out_ref.shape[0]):
        out_ref[r] = kv_ref[send_ref[r]]


def main_kernel(
    x_ref, wq_ref, wo_ref, cot_ref, kv_ref,
    slot_ref, keep_ref, send_ref, out_keep_ref, out_send_ref,
    w_ref, mixt_ref, gqt_ref, acc_ref,
):
    graph, mp = lax.axis_index("graph"), lax.axis_index("mp")
    tokens, width = x_ref.shape
    head_width = wq_ref.shape[1]
    groups = head_width // DH
    scale = DH ** (-0.5)
    query = (dot(x_ref[...], wq_ref[...]) * scale).astype(BF16)
    query_t = query.T
    grad_mixed_t = dot(wo_ref[...], cot_ref[...], NT).astype(BF16)
    w_ref[...] = jnp.zeros_like(w_ref)
    for k in range(groups):
        w_ref[k, :DH, :tokens] = query_t[k * DH : (k + 1) * DH]
        w_ref[k, DH:, tokens:] = grad_mixed_t[k * DH : (k + 1) * DH]
    kv = kv_ref[...]
    kv_t = kv.T
    acc_ref[...] = jnp.zeros_like(acc_ref)

    def group(k, carry):
        weights = w_ref[k]
        both = dot(kv, weights)
        score, grad_prob = both[:, :tokens], both[:, tokens:]
        exponent = jnp.exp(score - jnp.max(score, axis=0, keepdims=True))
        prob = exponent * (1.0 / jnp.sum(exponent, axis=0, keepdims=True))
        delta = jnp.sum(prob * grad_prob, axis=0, keepdims=True)
        rounded = prob.astype(BF16)
        grad_score = (prob * (grad_prob - delta)).astype(BF16)
        pair = jnp.concatenate([grad_score, rounded], axis=1)
        outs = dot(kv_t, pair)
        gqt_ref[k] = (outs[:DH, :tokens] * scale).astype(BF16)
        mixt_ref[k] = outs[DH:, tokens:].astype(BF16)
        acc_ref[...] += dot(pair, weights, NT)
        return carry

    lax.fori_loop(0, groups, group, 0)
    slot_ref[...] = acc_ref[...].astype(BF16)

    mixed_t = mixt_ref[...].reshape(head_width, tokens)
    grad_query_t = gqt_ref[...].reshape(head_width, tokens)
    y = lax.rem(graph, 2)
    z = lax.div(graph, 2)
    cols = keep_ref.shape[2]
    for d in range(keep_ref.shape[0]):
        base = lax.bitwise_xor(z, d) * 2
        for ref, index in ((keep_ref, base + y), (send_ref, base + 1 - y)):
            at = pl.ds(pl.multiple_of(index * cols, cols), cols)
            ref[d, :head_width] = dot(mixed_t, cot_ref[:, at])
            ref[d, head_width:] = dot(grad_query_t, x_ref[:, at])

    core = lax.rem(mp, 2)
    across = lax.div(mp, 2)
    mixed = mixed_t.T
    mixt_rows = out_keep_ref.shape[1]
    part = dot(mixed, wo_ref[...])
    for m in range(4):
        block = part[m * mixt_rows : (m + 1) * mixt_rows]
        place = lax.bitwise_xor(m // 2, across)

        @pl.when(core == m % 2)
        def _():
            out_keep_ref[place] = block

        @pl.when(core != m % 2)
        def _():
            out_send_ref[place] = block


def owner_kernel(send_ref, ret_ref, x_ref, out_ref):
    receivers, rows = ret_ref.shape[:2]
    tiles = x_ref.shape[0] // rows
    sums = []
    for t in range(tiles):
        total = jnp.zeros(ret_ref.shape[1:], F32)
        for r in range(receivers):
            mine = (send_ref[r] == t).astype(F32)
            total += ret_ref[r].astype(F32) * mine
        sums.append(total.astype(BF16))
    grad_kv_t = jnp.concatenate(sums, axis=0).T
    cols = out_ref.shape[2]
    whole = dot(grad_kv_t, x_ref[...])
    for r in range(out_ref.shape[0]):
        out_ref[r] = whole[:, r * cols : (r + 1) * cols]


def add_kernel(keep_ref, got_ref, *out_refs):
    for d, ref in enumerate(out_refs):
        ref[...] = keep_ref[d] + got_ref[d]


def final_kernel(own_ref, a_ref, b_ref, c_ref, kv_ref, wq_ref, wkv_ref, wo_ref):
    total = (own_ref[...] + a_ref[...]) + (b_ref[...] + c_ref[...])
    half = wo_ref.shape[0]
    wo_ref[...] = total[:half]
    wq_ref[...] = total[half:].T
    kv = kv_ref[0]
    for r in range(1, kv_ref.shape[0]):
        kv = kv + kv_ref[r]
    wkv_ref[...] = kv.T


def vmem(count):
    return [pl.BlockSpec(memory_space=pltpu.VMEM)] * count


SMEM = pl.BlockSpec(memory_space=pltpu.SMEM)


def xor_pairs(n, k):
    return [(i, i ^ k) for i in range(n)]


def shared_local(node_features, wq, wkv, wo, send_list, block_list, cotangent):
    tiles, rows, width = node_features.shape
    tokens = tiles * rows
    head_width = wq.shape[1] * wq.shape[2]
    kv_width = wkv.shape[2]
    groups = head_width // DH
    parts = lax.axis_size("graph")
    mp = lax.axis_size("mp")
    cols = width // parts
    x = node_features.reshape(tokens, width)
    send = send_list.reshape(-1)
    wq2, wkv2 = wq.reshape(width, head_width), wkv.reshape(width, kv_width)
    wo2 = wo.reshape(head_width, width)

    outgoing = pl.pallas_call(
        keyval_kernel,
        out_shape=jax.ShapeDtypeStruct((parts, rows, kv_width), BF16),
        in_specs=[SMEM] + vmem(2),
        out_specs=vmem(1)[0],
        scratch_shapes=[pltpu.VMEM((tiles, rows, kv_width), BF16)],
        name="keyval",
    )(send, x, wkv2)
    received = lax.all_to_all(outgoing, "graph", split_axis=0, concat_axis=0, tiled=True)
    keys = parts * rows
    share = tokens // mp
    outer = parts // 2
    slot_grad, keep, away, out_keep, out_away = pl.pallas_call(
        main_kernel,
        out_shape=(
            jax.ShapeDtypeStruct((keys, kv_width), BF16),
            jax.ShapeDtypeStruct((outer, 2 * head_width, cols), F32),
            jax.ShapeDtypeStruct((outer, 2 * head_width, cols), F32),
            jax.ShapeDtypeStruct((mp // 2, share, width), F32),
            jax.ShapeDtypeStruct((mp // 2, share, width), F32),
        ),
        in_specs=vmem(5),
        out_specs=tuple(vmem(5)),
        scratch_shapes=[
            pltpu.VMEM((groups, kv_width, 2 * tokens), BF16),
            pltpu.VMEM((groups, DH, tokens), BF16),
            pltpu.VMEM((groups, DH, tokens), BF16),
            pltpu.VMEM((keys, kv_width), F32),
        ],
        name="main",
    )(x, wq2, wo2, cotangent, received.reshape(keys, kv_width))

    got = lax.ppermute(away, "graph", xor_pairs(parts, 1))
    out_got = lax.ppermute(out_away, "mp", xor_pairs(mp, 1))
    returned = lax.all_to_all(
        slot_grad.reshape(parts, rows, kv_width), "graph", split_axis=0, concat_axis=0, tiled=True
    )
    kv_parts = pl.pallas_call(
        owner_kernel,
        out_shape=jax.ShapeDtypeStruct((parts, kv_width, cols), F32),
        in_specs=[SMEM] + vmem(2),
        out_specs=vmem(1)[0],
        name="owner",
    )(send, returned, x)
    out_half = out_keep + out_got
    out_last = lax.ppermute(out_half[1], "mp", xor_pairs(mp, 2))
    sums = pl.pallas_call(
        add_kernel,
        out_shape=tuple(jax.ShapeDtypeStruct(keep.shape[1:], F32) for _ in range(outer)),
        in_specs=vmem(2),
        out_specs=tuple(vmem(outer)),
        name="halves",
    )(keep, got)
    arrived = [lax.ppermute(sums[d], "graph", xor_pairs(parts, 2 * d)) for d in range(1, outer)]
    kv_got = lax.all_to_all(kv_parts, "graph", split_axis=0, concat_axis=0, tiled=True)
    own_rows = lax.dynamic_slice_in_dim(x, lax.axis_index("mp") * share, share, 0)
    output = (own_rows.astype(F32) + (out_half[0] + out_last)).astype(BF16)
    grad_wq, grad_wkv, grad_wo = pl.pallas_call(
        final_kernel,
        out_shape=(
            jax.ShapeDtypeStruct((cols, head_width), F32),
            jax.ShapeDtypeStruct((cols, kv_width), F32),
            jax.ShapeDtypeStruct((head_width, cols), F32),
        ),
        in_specs=vmem(5),
        out_specs=tuple(vmem(3)),
        name="final",
    )(sums[0], *arrived, kv_got)
    return (
        output,
        grad_wq.reshape(cols, *wq.shape[1:]),
        grad_wkv.reshape(cols, *wkv.shape[1:]),
        grad_wo.reshape(*wo.shape[:2], cols),
    )


def local(node_features, wq, wkv, wo, send_list, block_list, cotangent):
    parts, mp, slots = lax.axis_size("graph"), lax.axis_size("mp"), send_list.shape[2]
    copies, rest = divmod(block_list.shape[1], parts * slots)
    every_slot = rest == 0 and copies & (copies - 1) == 0
    if every_slot and slots == 1 and parts == 8 and mp == 4 and wq.shape[1] == 1:
        body = shared_local
    else:
        body = listed_local
    return body(node_features, wq, wkv, wo, send_list, block_list, cotangent)


def solution(mesh):
    return jax.shard_map(
        local,
        mesh=mesh,
        in_specs=(
            P("graph", None, None),
            P(None, "mp", None),
            P(None, "mp", None),
            P("mp", None, None),
            P("graph", None, None),
            P("graph", None),
            P("graph", None),
        ),
        out_specs=(
            P(("graph", "mp"), None),
            P("graph", "mp", None),
            P("graph", "mp", None),
            P("mp", None, "graph"),
        ),
        check_vma=False,
    )
```

```python
import jax
import jax.numpy as jnp
from jax import lax
from jax.experimental import pallas as pl
from jax.experimental.pallas import tpu as pltpu
from jax.sharding import PartitionSpec as P

DH = 64
F32 = jnp.float32
BF16 = jnp.bfloat16


def head_forward(query_head, key_flat, width):
    score = jnp.einsum(
        "rhd,khd->hrk", query_head, key_flat[..., :width], preferred_element_type=F32
    )
    row_max = jnp.max(score, axis=-1, keepdims=True)
    exponent = jnp.exp(score - row_max)
    weights = exponent / jnp.sum(exponent, axis=-1, keepdims=True)
    rounded = weights.astype(BF16)
    mixed = jnp.einsum(
        "hrk,khd->rhd", rounded, key_flat[..., width:], preferred_element_type=F32
    ).astype(BF16)
    return (weights, rounded, mixed)


def tile_forward(query_tile, key_rows):
    heads = query_tile.shape[1]
    width = query_tile.shape[3]
    key_flat = key_rows.reshape(-1, heads, 2 * width)

    def one_head(query_head):
        return head_forward(query_head, key_flat, width)[2]

    per_head = lax.map(one_head, jnp.moveaxis(query_tile, 2, 0))
    return jnp.moveaxis(per_head, 0, 2)


def tile_backward(query_tile, key_rows, grad_tile):
    heads = query_tile.shape[1]
    width = query_tile.shape[3]
    key_flat = key_rows.reshape(-1, heads, 2 * width)

    def one_head(total, entry):
        query_head, grad_head = entry
        weights, rounded, _ = head_forward(query_head, key_flat, width)
        grad_prob = jnp.einsum(
            "rhd,khd->hrk", grad_head, key_flat[..., width:], preferred_element_type=F32
        )
        delta = jnp.sum(weights * grad_prob, axis=-1, keepdims=True)
        grad_score = (weights * (grad_prob - delta)).astype(BF16)
        grad_query = (
            jnp.einsum(
                "hrk,khd->rhd", grad_score, key_flat[..., :width], preferred_element_type=F32
            )
            * width ** (-0.5)
        ).astype(BF16)
        grad_key = jnp.einsum("hrk,rhd->khd", grad_score, query_head, preferred_element_type=F32)
        grad_value = jnp.einsum("hrk,rhd->khd", rounded, grad_head, preferred_element_type=F32)
        total = total + jnp.concatenate([grad_key, grad_value], axis=-1)
        return (total, grad_query)

    start_total = jnp.zeros(key_flat.shape, F32)
    key_grad, grad_query = lax.scan(
        one_head, start_total, (jnp.moveaxis(query_tile, 2, 0), jnp.moveaxis(grad_tile, 2, 0))
    )
    return (jnp.moveaxis(grad_query, 0, 2), key_grad.reshape(key_rows.shape))


def listed_local(node_features, wq, wkv, wo, send_list, block_list, cotangent):
    tiles, tile_rows, width = node_features.shape
    heads = wq.shape[1]
    head_width = wq.shape[2]
    groups = head_width // DH
    parts = lax.axis_size("graph")
    slots = send_list.shape[2]
    token_rows = node_features.reshape(tiles * tile_rows, width)
    query = (
        jnp.dot(token_rows, wq.reshape(width, -1), preferred_element_type=F32) * DH ** (-0.5)
    ).astype(BF16)
    query = query.reshape(tiles, tile_rows, heads, groups, DH)
    keyval = jnp.dot(token_rows, wkv.reshape(width, -1), preferred_element_type=F32).astype(BF16)
    keyval = keyval.reshape(tiles, tile_rows, -1)
    outgoing = keyval[send_list[0].reshape(-1)]
    received = lax.all_to_all(outgoing, "graph", split_axis=0, concat_axis=0, tiled=True)

    def forward_one(entry):
        query_tile, key_ids = entry
        return tile_forward(query_tile, received[key_ids])

    mixed = lax.map(forward_one, (query, block_list))
    mixed_rows = mixed.reshape(tiles * tile_rows, heads * head_width)
    out_flat = wo.reshape(heads * head_width, width)
    share = tiles * tile_rows // lax.axis_size("mp")
    summed = lax.psum_scatter(
        jnp.dot(mixed_rows, out_flat, preferred_element_type=F32),
        "mp",
        scatter_dimension=0,
        tiled=True,
    )
    own_rows = lax.dynamic_slice_in_dim(token_rows, lax.axis_index("mp") * share, share, 0)
    output = (own_rows.astype(F32) + summed).astype(BF16)
    grad_out_local = jnp.dot(mixed_rows.T, cotangent, preferred_element_type=F32).reshape(wo.shape)
    grad_mixed = jnp.einsum("rd,hd->rh", cotangent, out_flat, preferred_element_type=F32).astype(
        BF16
    )
    grad_mixed = grad_mixed.reshape(tiles, tile_rows, heads, groups, DH)

    def backward_one(entry):
        query_tile, key_ids, grad_tile = entry
        return tile_backward(query_tile, received[key_ids], grad_tile)

    grad_query, key_grad = lax.map(backward_one, (query, block_list, grad_mixed))
    slot_ids = jnp.arange(parts * slots, dtype=jnp.int32)
    picks = (block_list.reshape(1, -1) == slot_ids[:, None]).astype(F32)
    slot_grad = jnp.dot(
        picks,
        key_grad.reshape(tiles * block_list.shape[1], -1),
        precision=lax.Precision.HIGHEST,
        preferred_element_type=F32,
    ).astype(BF16)
    slot_grad = slot_grad.reshape(parts * slots, tile_rows, -1)
    returned = lax.all_to_all(slot_grad, "graph", split_axis=0, concat_axis=0, tiled=True)
    owners = (send_list[0].reshape(1, -1) == jnp.arange(tiles, dtype=jnp.int32)[:, None]).astype(
        BF16
    )
    grad_keyval = jnp.dot(
        owners, returned.reshape(parts * slots, -1), preferred_element_type=F32
    ).astype(BF16)
    grad_keyval = grad_keyval.reshape(tiles * tile_rows, -1)
    grad_query_local = jnp.dot(
        token_rows.T, grad_query.reshape(tiles * tile_rows, -1), preferred_element_type=F32
    ).reshape(wq.shape)
    grad_keyval_local = jnp.dot(token_rows.T, grad_keyval, preferred_element_type=F32).reshape(
        wkv.shape
    )
    grad_wq = lax.psum_scatter(grad_query_local, "graph", scatter_dimension=0, tiled=True)
    grad_wkv = lax.psum_scatter(grad_keyval_local, "graph", scatter_dimension=0, tiled=True)
    grad_out = lax.psum_scatter(grad_out_local, "graph", scatter_dimension=2, tiled=True)
    return (output, grad_wq, grad_wkv, grad_out)


def dot(a, b, contract=((1,), (0,))):
    return lax.dot_general(a, b, (contract, ((), ())), preferred_element_type=F32)


NT = ((1,), (1,))


def keyval_kernel(send_ref, x_ref, wkv_ref, out_ref, kv_ref):
    rows = out_ref.shape[1]
    kv = dot(x_ref[...], wkv_ref[...]).astype(BF16)
    for t in range(kv_ref.shape[0]):
        kv_ref[t] = kv[t * rows : (t + 1) * rows]
    for r in range(out_ref.shape[0]):
        out_ref[r] = kv_ref[send_ref[r]]


def project_kernel(x_ref, wq_ref, wo_ref, cot_ref, w_ref, half_ref):
    tokens = x_ref.shape[0]
    groups = w_ref.shape[0]
    query = (dot(x_ref[...], wq_ref[...]) * DH ** (-0.5)).astype(BF16)
    query_t = query.T
    grad_mixed_t = dot(wo_ref[...], cot_ref[...], NT).astype(BF16)
    w_ref[...] = jnp.zeros_like(w_ref)
    for k in range(groups):
        w_ref[k, :DH, :tokens] = query_t[k * DH : (k + 1) * DH]
        w_ref[k, DH:, tokens:] = grad_mixed_t[k * DH : (k + 1) * DH]
    other = 1 - lax.rem(lax.axis_index("graph"), 2)
    outer = half_ref.shape[1]
    cols = half_ref.shape[3]
    for d in range(outer):
        at = pl.ds(pl.multiple_of((2 * d + other) * cols, cols), cols)
        half_ref[0, d] = cot_ref[:, at]
        half_ref[1, d] = x_ref[:, at]


def attention_kernel(w_ref, kv_ref, slot_ref, mix_ref, acc_ref):
    groups, _, twice = w_ref.shape
    tokens = twice // 2
    scale = DH ** (-0.5)
    kv = kv_ref[...]
    kv_t = kv.T
    acc_ref[...] = jnp.zeros_like(acc_ref)

    def group(k, carry):
        weights = w_ref[k]
        both = dot(kv, weights)
        score, grad_prob = both[:, :tokens], both[:, tokens:]
        exponent = jnp.exp(score - jnp.max(score, axis=0, keepdims=True))
        prob = exponent * (1.0 / jnp.sum(exponent, axis=0, keepdims=True))
        delta = jnp.sum(prob * grad_prob, axis=0, keepdims=True)
        rounded = prob.astype(BF16)
        grad_score = (prob * (grad_prob - delta)).astype(BF16)
        pair = jnp.concatenate([grad_score, rounded], axis=1)
        outs = dot(kv_t, pair)
        mix_ref[0, k] = outs[DH:, tokens:].astype(BF16)
        mix_ref[1, k] = (outs[:DH, :tokens] * scale).astype(BF16)
        acc_ref[...] += dot(pair, weights, NT)
        return carry

    lax.fori_loop(0, groups, group, 0)
    slot_ref[...] = acc_ref[...].astype(BF16)


def output_kernel(mix_ref, wo_ref, out_keep_ref, out_send_ref):
    mp = lax.axis_index("mp")
    core, across = lax.rem(mp, 2), lax.div(mp, 2)
    rows = out_keep_ref.shape[1]
    mixed = mix_ref[0].T
    part = dot(mixed, wo_ref[...])
    for m in range(4):
        block = part[m * rows : (m + 1) * rows]
        place = lax.bitwise_xor(m // 2, across)

        @pl.when(core == m % 2)
        def _():
            out_keep_ref[place] = block

        @pl.when(core != m % 2)
        def _():
            out_send_ref[place] = block


def exponent_of(peak):
    return jnp.ceil(jnp.log2(jnp.maximum(peak, 1e-30))) - 14.0


def peak_of(value, peak):
    top = jnp.max(jnp.abs(value), axis=0, keepdims=True)
    return jnp.maximum(peak, jnp.max(top, axis=1, keepdims=True))


def weights_kernel(mix_ref, mix_got_ref, cot_ref, x_ref, half_ref, own_ref, *out_refs):
    graph = lax.axis_index("graph")
    y, z = lax.rem(graph, 2), lax.div(graph, 2)
    head_width = mix_ref.shape[1]
    cols = half_ref.shape[3]
    parts = head_width // cols
    refs = (own_ref,) + out_refs
    peak = jnp.zeros((1, 1), F32)
    for d, ref in enumerate(refs):
        there = lax.bitwise_xor(z, d)
        at = pl.ds(pl.multiple_of((2 * there + y) * cols, cols), cols)
        wo = dot(mix_ref[0], cot_ref[:, at]) + dot(mix_got_ref[0], half_ref[0, there])
        wq = dot(mix_ref[1], x_ref[:, at]) + dot(mix_got_ref[1], half_ref[1, there])
        ref[:head_width] = wo
        for h in range(parts):
            place = pl.ds(head_width + h, cols, parts)
            ref[place, :] = wq[h * cols : (h + 1) * cols].T
        if d > 0:
            peak = peak_of(wo, peak_of(wq, peak))
    e = exponent_of(peak)
    factor = jnp.exp2(-e)
    rows = 2 * head_width
    for ref in out_refs:
        ref[:rows] = ref[:rows] * factor
        ref[rows:] = jnp.broadcast_to(e, ref[rows:].shape)


def owner_kernel(send_ref, ret_ref, x_ref, out_ref):
    receivers, rows = ret_ref.shape[:2]
    tiles = x_ref.shape[0] // rows
    sums = []
    for t in range(tiles):
        total = jnp.zeros(ret_ref.shape[1:], F32)
        for r in range(receivers):
            mine = (send_ref[r] == t).astype(F32)
            total += ret_ref[r].astype(F32) * mine
        sums.append(total.astype(BF16))
    grad_kv_t = jnp.concatenate(sums, axis=0).T
    cols = out_ref.shape[2]
    kv_width = grad_kv_t.shape[0]
    whole = dot(grad_kv_t, x_ref[...])
    e = exponent_of(peak_of(whole, jnp.zeros((1, 1), F32)))
    factor = jnp.exp2(-e)
    for r in range(out_ref.shape[0]):
        out_ref[r, :kv_width] = whole[:, r * cols : (r + 1) * cols].T * factor
        out_ref[r, kv_width:] = jnp.broadcast_to(e, out_ref[r, kv_width:].shape)


def unscaled(got):
    rows = got.shape[-2] - 16
    return got[..., :rows, :].astype(F32) * jnp.exp2(got[..., rows : rows + 1, :1].astype(F32))


def vmem(count):
    return [pl.BlockSpec(memory_space=pltpu.VMEM)] * count


SMEM = pl.BlockSpec(memory_space=pltpu.SMEM)


def xor_pairs(n, k):
    return [(i, i ^ k) for i in range(n)]


def shared_local(node_features, wq, wkv, wo, send_list, block_list, cotangent):
    tiles, rows, width = node_features.shape
    tokens = tiles * rows
    head_width = wq.shape[1] * wq.shape[2]
    kv_width = wkv.shape[2]
    groups = head_width // DH
    parts = lax.axis_size("graph")
    mp = lax.axis_size("mp")
    cols = width // parts
    x = node_features.reshape(tokens, width)
    send = send_list.reshape(-1)
    wq2, wkv2 = wq.reshape(width, head_width), wkv.reshape(width, kv_width)
    wo2 = wo.reshape(head_width, width)

    outgoing = pl.pallas_call(
        keyval_kernel,
        out_shape=jax.ShapeDtypeStruct((parts, rows, kv_width), BF16),
        in_specs=[SMEM] + vmem(2),
        out_specs=vmem(1)[0],
        scratch_shapes=[pltpu.VMEM((tiles, rows, kv_width), BF16)],
        name="keyval",
    )(send, x, wkv2)
    received = lax.all_to_all(outgoing, "graph", split_axis=0, concat_axis=0, tiled=True)
    keys = parts * rows
    share = tokens // mp
    outer = parts // 2
    weights, half = pl.pallas_call(
        project_kernel,
        out_shape=(
            jax.ShapeDtypeStruct((groups, kv_width, 2 * tokens), BF16),
            jax.ShapeDtypeStruct((2, outer, tokens, cols), BF16),
        ),
        in_specs=vmem(4),
        out_specs=tuple(vmem(2)),
        name="project",
    )(x, wq2, wo2, cotangent)
    half_got = lax.ppermute(half, "graph", xor_pairs(parts, 1))
    slot_grad, mix = pl.pallas_call(
        attention_kernel,
        out_shape=(
            jax.ShapeDtypeStruct((keys, kv_width), BF16),
            jax.ShapeDtypeStruct((2, groups, DH, tokens), BF16),
        ),
        in_specs=vmem(2),
        out_specs=tuple(vmem(2)),
        scratch_shapes=[pltpu.VMEM((keys, kv_width), F32)],
        name="attention",
    )(weights, received.reshape(keys, kv_width))
    returned = lax.all_to_all(
        slot_grad.reshape(parts, rows, kv_width), "graph", split_axis=0, concat_axis=0, tiled=True
    )
    mix = mix.reshape(2, head_width, tokens)
    mix_got = lax.ppermute(mix, "graph", xor_pairs(parts, 1))
    out_keep, out_away = pl.pallas_call(
        output_kernel,
        out_shape=(
            jax.ShapeDtypeStruct((mp // 2, share, width), F32),
            jax.ShapeDtypeStruct((mp // 2, share, width), F32),
        ),
        in_specs=vmem(2),
        out_specs=tuple(vmem(2)),
        name="output",
    )(mix, wo2)
    out_got = lax.ppermute(out_away, "mp", xor_pairs(mp, 1))
    sums, *sums_away = pl.pallas_call(
        weights_kernel,
        out_shape=tuple(
            jax.ShapeDtypeStruct((2 * head_width + 16 * (d > 0), cols), F32)
            for d in range(outer)
        ),
        in_specs=vmem(5),
        out_specs=tuple(vmem(outer)),
        name="weights",
    )(mix, mix_got, cotangent, x, half_got)
    sums_got = []
    for d in range(1, outer):
        away = sums_away[d - 1].astype(jnp.float16)
        sums_got.append(lax.ppermute(away, "graph", xor_pairs(parts, 2 * d)))
    kv_parts = pl.pallas_call(
        owner_kernel,
        out_shape=jax.ShapeDtypeStruct((parts, kv_width + 16, cols), F32),
        in_specs=[SMEM] + vmem(2),
        out_specs=vmem(1)[0],
        name="owner",
    )(send, returned, x)
    kv_parts = kv_parts.astype(jnp.float16)
    kv_got = lax.all_to_all(kv_parts, "graph", split_axis=0, concat_axis=0, tiled=True)
    out_half = out_keep + out_got
    out_last = lax.ppermute(out_half[1], "mp", xor_pairs(mp, 2))
    own_rows = lax.dynamic_slice_in_dim(x, lax.axis_index("mp") * share, share, 0)
    output = (own_rows.astype(F32) + (out_half[0] + out_last)).astype(BF16)
    for got in sums_got:
        sums = sums + unscaled(got)
    grad_wo, grad_wq = sums[:head_width], sums[head_width:]
    grad_wkv = jnp.sum(unscaled(kv_got), axis=0)
    return (
        output,
        grad_wq.reshape(cols, *wq.shape[1:]),
        grad_wkv.reshape(cols, *wkv.shape[1:]),
        grad_wo.reshape(*wo.shape[:2], cols),
    )


def local(node_features, wq, wkv, wo, send_list, block_list, cotangent):
    parts, mp, slots = lax.axis_size("graph"), lax.axis_size("mp"), send_list.shape[2]
    copies, rest = divmod(block_list.shape[1], parts * slots)
    every_slot = rest == 0 and copies & (copies - 1) == 0
    if every_slot and slots == 1 and parts == 8 and mp == 4 and wq.shape[1] == 1:
        body = shared_local
    else:
        body = listed_local
    return body(node_features, wq, wkv, wo, send_list, block_list, cotangent)


def solution(mesh):
    return jax.shard_map(
        local,
        mesh=mesh,
        in_specs=(
            P("graph", None, None),
            P(None, "mp", None),
            P(None, "mp", None),
            P("mp", None, None),
            P("graph", None, None),
            P("graph", None),
            P("graph", None),
        ),
        out_specs=(
            P(("graph", "mp"), None),
            P("graph", "mp", None),
            P("graph", "mp", None),
            P("mp", None, "graph"),
        ),
        check_vma=False,
    )
```

```python
import jax
import jax.numpy as jnp
from jax import lax
from jax.experimental import pallas as pl
from jax.experimental.pallas import tpu as pltpu
from jax.sharding import PartitionSpec as P

DH = 64
F32 = jnp.float32
BF16 = jnp.bfloat16


def head_forward(query_head, key_flat, width):
    score = jnp.einsum(
        "rhd,khd->hrk", query_head, key_flat[..., :width], preferred_element_type=F32
    )
    row_max = jnp.max(score, axis=-1, keepdims=True)
    exponent = jnp.exp(score - row_max)
    weights = exponent / jnp.sum(exponent, axis=-1, keepdims=True)
    rounded = weights.astype(BF16)
    mixed = jnp.einsum(
        "hrk,khd->rhd", rounded, key_flat[..., width:], preferred_element_type=F32
    ).astype(BF16)
    return (weights, rounded, mixed)


def tile_forward(query_tile, key_rows):
    heads = query_tile.shape[1]
    width = query_tile.shape[3]
    key_flat = key_rows.reshape(-1, heads, 2 * width)

    def one_head(query_head):
        return head_forward(query_head, key_flat, width)[2]

    per_head = lax.map(one_head, jnp.moveaxis(query_tile, 2, 0))
    return jnp.moveaxis(per_head, 0, 2)


def tile_backward(query_tile, key_rows, grad_tile):
    heads = query_tile.shape[1]
    width = query_tile.shape[3]
    key_flat = key_rows.reshape(-1, heads, 2 * width)

    def one_head(total, entry):
        query_head, grad_head = entry
        weights, rounded, _ = head_forward(query_head, key_flat, width)
        grad_prob = jnp.einsum(
            "rhd,khd->hrk", grad_head, key_flat[..., width:], preferred_element_type=F32
        )
        delta = jnp.sum(weights * grad_prob, axis=-1, keepdims=True)
        grad_score = (weights * (grad_prob - delta)).astype(BF16)
        grad_query = (
            jnp.einsum(
                "hrk,khd->rhd", grad_score, key_flat[..., :width], preferred_element_type=F32
            )
            * width ** (-0.5)
        ).astype(BF16)
        grad_key = jnp.einsum("hrk,rhd->khd", grad_score, query_head, preferred_element_type=F32)
        grad_value = jnp.einsum("hrk,rhd->khd", rounded, grad_head, preferred_element_type=F32)
        total = total + jnp.concatenate([grad_key, grad_value], axis=-1)
        return (total, grad_query)

    start_total = jnp.zeros(key_flat.shape, F32)
    key_grad, grad_query = lax.scan(
        one_head, start_total, (jnp.moveaxis(query_tile, 2, 0), jnp.moveaxis(grad_tile, 2, 0))
    )
    return (jnp.moveaxis(grad_query, 0, 2), key_grad.reshape(key_rows.shape))


def listed_local(node_features, wq, wkv, wo, send_list, block_list, cotangent):
    tiles, tile_rows, width = node_features.shape
    heads = wq.shape[1]
    head_width = wq.shape[2]
    groups = head_width // DH
    parts = lax.axis_size("graph")
    slots = send_list.shape[2]
    token_rows = node_features.reshape(tiles * tile_rows, width)
    query = (
        jnp.dot(token_rows, wq.reshape(width, -1), preferred_element_type=F32) * DH ** (-0.5)
    ).astype(BF16)
    query = query.reshape(tiles, tile_rows, heads, groups, DH)
    keyval = jnp.dot(token_rows, wkv.reshape(width, -1), preferred_element_type=F32).astype(BF16)
    keyval = keyval.reshape(tiles, tile_rows, -1)
    outgoing = keyval[send_list[0].reshape(-1)]
    received = lax.all_to_all(outgoing, "graph", split_axis=0, concat_axis=0, tiled=True)

    def forward_one(entry):
        query_tile, key_ids = entry
        return tile_forward(query_tile, received[key_ids])

    mixed = lax.map(forward_one, (query, block_list))
    mixed_rows = mixed.reshape(tiles * tile_rows, heads * head_width)
    out_flat = wo.reshape(heads * head_width, width)
    share = tiles * tile_rows // lax.axis_size("mp")
    summed = lax.psum_scatter(
        jnp.dot(mixed_rows, out_flat, preferred_element_type=F32),
        "mp",
        scatter_dimension=0,
        tiled=True,
    )
    own_rows = lax.dynamic_slice_in_dim(token_rows, lax.axis_index("mp") * share, share, 0)
    output = (own_rows.astype(F32) + summed).astype(BF16)
    grad_out_local = jnp.dot(mixed_rows.T, cotangent, preferred_element_type=F32).reshape(wo.shape)
    grad_mixed = jnp.einsum("rd,hd->rh", cotangent, out_flat, preferred_element_type=F32).astype(
        BF16
    )
    grad_mixed = grad_mixed.reshape(tiles, tile_rows, heads, groups, DH)

    def backward_one(entry):
        query_tile, key_ids, grad_tile = entry
        return tile_backward(query_tile, received[key_ids], grad_tile)

    grad_query, key_grad = lax.map(backward_one, (query, block_list, grad_mixed))
    slot_ids = jnp.arange(parts * slots, dtype=jnp.int32)
    picks = (block_list.reshape(1, -1) == slot_ids[:, None]).astype(F32)
    slot_grad = jnp.dot(
        picks,
        key_grad.reshape(tiles * block_list.shape[1], -1),
        precision=lax.Precision.HIGHEST,
        preferred_element_type=F32,
    ).astype(BF16)
    slot_grad = slot_grad.reshape(parts * slots, tile_rows, -1)
    returned = lax.all_to_all(slot_grad, "graph", split_axis=0, concat_axis=0, tiled=True)
    owners = (send_list[0].reshape(1, -1) == jnp.arange(tiles, dtype=jnp.int32)[:, None]).astype(
        BF16
    )
    grad_keyval = jnp.dot(
        owners, returned.reshape(parts * slots, -1), preferred_element_type=F32
    ).astype(BF16)
    grad_keyval = grad_keyval.reshape(tiles * tile_rows, -1)
    grad_query_local = jnp.dot(
        token_rows.T, grad_query.reshape(tiles * tile_rows, -1), preferred_element_type=F32
    ).reshape(wq.shape)
    grad_keyval_local = jnp.dot(token_rows.T, grad_keyval, preferred_element_type=F32).reshape(
        wkv.shape
    )
    grad_wq = lax.psum_scatter(grad_query_local, "graph", scatter_dimension=0, tiled=True)
    grad_wkv = lax.psum_scatter(grad_keyval_local, "graph", scatter_dimension=0, tiled=True)
    grad_out = lax.psum_scatter(grad_out_local, "graph", scatter_dimension=2, tiled=True)
    return (output, grad_wq, grad_wkv, grad_out)


def dot(a, b, contract=((1,), (0,))):
    return lax.dot_general(a, b, (contract, ((), ())), preferred_element_type=F32)


NT = ((1,), (1,))


def keyval_kernel(send_hbm, x_hbm, wkv_hbm, out_ref, x_ref, wkv_ref, send_ref, kv_ref, sems):
    rows = out_ref.shape[1]
    chunks = sems.shape[1]
    depth = x_ref.shape[1] // chunks
    copies = []
    for c in range(chunks):
        at = pl.ds(c * depth, depth)
        pair = (
            pltpu.make_async_copy(x_hbm.at[:, at], x_ref.at[:, at], sems.at[0, c]),
            pltpu.make_async_copy(wkv_hbm.at[at], wkv_ref.at[at], sems.at[1, c]),
        )
        for copy in pair:
            copy.start()
        copies.append(pair)
    listing = pltpu.make_async_copy(send_hbm, send_ref, sems.at[2, 0])
    listing.start()
    kv = None
    for c, pair in enumerate(copies):
        for copy in pair:
            copy.wait()
        at = pl.ds(c * depth, depth)
        part = dot(x_ref[:, at], wkv_ref[at])
        kv = part if kv is None else kv + part
    kv = kv.astype(BF16)
    for t in range(kv_ref.shape[0]):
        kv_ref[t] = kv[t * rows : (t + 1) * rows]
    listing.wait()
    for r in range(out_ref.shape[0]):
        out_ref[r] = kv_ref[send_ref[r]]


def project_kernel(x_ref, wq_ref, wo_ref, cot_ref, w_ref):
    tokens = x_ref.shape[0]
    groups = w_ref.shape[0]
    query = (dot(x_ref[...], wq_ref[...]) * DH ** (-0.5)).astype(BF16)
    query_t = query.T
    grad_mixed_t = dot(wo_ref[...], cot_ref[...], NT).astype(BF16)
    w_ref[...] = jnp.zeros_like(w_ref)
    for k in range(groups):
        w_ref[k, :DH, :tokens] = query_t[k * DH : (k + 1) * DH]
        w_ref[k, DH:, tokens:] = grad_mixed_t[k * DH : (k + 1) * DH]


def halves_kernel(cot_ref, x_ref, half_ref):
    other = 1 - lax.rem(lax.axis_index("graph"), 2)
    outer = half_ref.shape[1]
    cols = half_ref.shape[3]
    for d in range(outer):
        at = pl.ds(pl.multiple_of((2 * d + other) * cols, cols), cols)
        half_ref[0, d] = cot_ref[:, at]
        half_ref[1, d] = x_ref[:, at]


def attention_kernel(w_ref, kv_ref, slot_ref, mix_ref, acc_ref, both_ref, pair_ref):
    groups, _, twice = w_ref.shape
    tokens = twice // 2
    scale = DH ** (-0.5)
    kv_t = kv_ref[...].T

    def scores(k):
        both = dot(kv_ref[...], w_ref[k])
        both_ref[k % 2] = both
        return jnp.max(both[:, :tokens], axis=0, keepdims=True)

    top = scores(0)
    for k in range(groups):
        b = k % 2
        exponent = jnp.exp(both_ref[b, :, :tokens] - top)
        grad_prob = both_ref[b, :, tokens:]
        inverse = 1.0 / jnp.sum(exponent, axis=0, keepdims=True)
        prob = exponent * inverse
        delta = jnp.sum(prob * grad_prob, axis=0, keepdims=True)
        pair_ref[b, :, tokens:] = prob.astype(BF16)
        pair_ref[b, :, :tokens] = (prob * (grad_prob - delta)).astype(BF16)
        if k + 1 < groups:
            top = scores(k + 1)
        outs = dot(kv_t, pair_ref[b])
        mix_ref[0, k] = outs[DH:, tokens:].astype(BF16)
        mix_ref[1, k] = (outs[:DH, :tokens] * scale).astype(BF16)
        grad = dot(pair_ref[b], w_ref[k], NT)
        if k == 0:
            acc_ref[...] = grad
        elif k + 1 < groups:
            acc_ref[...] += grad
        else:
            slot_ref[...] = (acc_ref[...] + grad).astype(BF16)


def output_kernel(mix_ref, wo_ref, out_keep_ref, out_send_ref):
    mp = lax.axis_index("mp")
    core, across = lax.rem(mp, 2), lax.div(mp, 2)
    rows = out_keep_ref.shape[1]
    mixed = mix_ref[0].T
    part = dot(mixed, wo_ref[...])
    for m in range(4):
        block = part[m * rows : (m + 1) * rows]
        place = lax.bitwise_xor(m // 2, across)

        @pl.when(core == m % 2)
        def _():
            out_keep_ref[place] = block

        @pl.when(core != m % 2)
        def _():
            out_send_ref[place] = block


def exponent_of(peak):
    return jnp.ceil(jnp.log2(jnp.maximum(peak, 1e-30))) - 14.0


def peak_of(value, peak):
    top = jnp.max(jnp.abs(value), axis=0, keepdims=True)
    return jnp.maximum(peak, jnp.max(top, axis=1, keepdims=True))


def weights_kernel(mix_ref, mix_got_ref, cot_ref, x_ref, half_ref, own_ref, *out_refs):
    graph = lax.axis_index("graph")
    y, z = lax.rem(graph, 2), lax.div(graph, 2)
    head_width = mix_ref.shape[1]
    cols = half_ref.shape[3]
    parts = head_width // cols
    refs = (own_ref,) + out_refs
    peak = jnp.zeros((1, 1), F32)
    for d, ref in enumerate(refs):
        there = lax.bitwise_xor(z, d)
        at = pl.ds(pl.multiple_of((2 * there + y) * cols, cols), cols)
        wo = dot(mix_ref[0], cot_ref[:, at]) + dot(mix_got_ref[0], half_ref[0, there])
        wq = dot(mix_ref[1], x_ref[:, at]) + dot(mix_got_ref[1], half_ref[1, there])
        ref[:head_width] = wo
        for h in range(parts):
            place = pl.ds(head_width + h, cols, parts)
            ref[place, :] = wq[h * cols : (h + 1) * cols].T
        if d > 0:
            peak = peak_of(wo, peak_of(wq, peak))
    e = exponent_of(peak)
    factor = jnp.exp2(-e)
    rows = 2 * head_width
    for ref in out_refs:
        ref[:rows] = ref[:rows] * factor
        ref[rows:] = jnp.broadcast_to(e, ref[rows:].shape)


def owner_kernel(send_ref, ret_ref, x_ref, out_ref):
    receivers, rows = ret_ref.shape[:2]
    tiles = x_ref.shape[0] // rows
    sums = []
    for t in range(tiles):
        total = jnp.zeros(ret_ref.shape[1:], F32)
        for r in range(receivers):
            mine = (send_ref[r] == t).astype(F32)
            total += ret_ref[r].astype(F32) * mine
        sums.append(total.astype(BF16))
    grad_kv_t = jnp.concatenate(sums, axis=0).T
    cols = out_ref.shape[2]
    kv_width = grad_kv_t.shape[0]
    whole = dot(grad_kv_t, x_ref[...])
    e = exponent_of(peak_of(whole, jnp.zeros((1, 1), F32)))
    factor = jnp.exp2(-e)
    for r in range(out_ref.shape[0]):
        out_ref[r, :kv_width] = whole[:, r * cols : (r + 1) * cols].T * factor
        out_ref[r, kv_width:] = jnp.broadcast_to(e, out_ref[r, kv_width:].shape)


def unscaled(value):
    rows = value.shape[0] - 16
    return value[:rows] * jnp.exp2(value[rows : rows + 1])


def sums_kernel(own_ref, *refs):
    *got_refs, wo_ref, wq_ref = refs
    total = own_ref[...]
    for ref in got_refs:
        total = total + unscaled(ref[...])
    half = wo_ref.shape[0]
    wo_ref[...] = total[:half]
    wq_ref[...] = total[half:]


def kvsum_kernel(got_ref, out_ref):
    total = unscaled(got_ref[0])
    for r in range(1, got_ref.shape[0]):
        total = total + unscaled(got_ref[r])
    out_ref[...] = total


GRANT = pltpu.CompilerParams(vmem_limit_bytes=8 << 20)
WIDE = pltpu.CompilerParams(vmem_limit_bytes=16 << 20)


def vmem(count):
    return [pl.BlockSpec(memory_space=pltpu.VMEM)] * count


SMEM = pl.BlockSpec(memory_space=pltpu.SMEM)


def xor_pairs(n, k):
    return [(i, i ^ k) for i in range(n)]


def shared_local(node_features, wq, wkv, wo, send_list, block_list, cotangent):
    tiles, rows, width = node_features.shape
    tokens = tiles * rows
    head_width = wq.shape[1] * wq.shape[2]
    kv_width = wkv.shape[2]
    groups = head_width // DH
    parts = lax.axis_size("graph")
    mp = lax.axis_size("mp")
    cols = width // parts
    x = node_features.reshape(tokens, width)
    send = send_list.reshape(-1)
    wq2, wkv2 = wq.reshape(width, head_width), wkv.reshape(width, kv_width)
    wo2 = wo.reshape(head_width, width)

    outgoing = pl.pallas_call(
        keyval_kernel,
        out_shape=jax.ShapeDtypeStruct((parts, rows, kv_width), BF16),
        in_specs=[pl.BlockSpec(memory_space=pltpu.HBM)] * 3,
        out_specs=vmem(1)[0],
        scratch_shapes=[
            pltpu.VMEM(x.shape, BF16),
            pltpu.VMEM(wkv2.shape, BF16),
            pltpu.SMEM(send.shape, jnp.int32),
            pltpu.VMEM((tiles, rows, kv_width), BF16),
            pltpu.SemaphoreType.DMA((3, 4)),
        ],
        name="keyval",
    )(send, x, wkv2)
    received = lax.all_to_all(outgoing, "graph", split_axis=0, concat_axis=0, tiled=True)
    keys = parts * rows
    share = tokens // mp
    outer = parts // 2
    weights = pl.pallas_call(
        project_kernel,
        out_shape=jax.ShapeDtypeStruct((groups, kv_width, 2 * tokens), BF16),
        in_specs=vmem(4),
        out_specs=vmem(1)[0],
        compiler_params=GRANT,
        name="project",
    )(x, wq2, wo2, cotangent)
    half = pl.pallas_call(
        halves_kernel,
        out_shape=jax.ShapeDtypeStruct((2, outer, tokens, cols), BF16),
        in_specs=vmem(2),
        out_specs=vmem(1)[0],
        compiler_params=GRANT,
        name="halves",
    )(cotangent, x)
    half_got = lax.ppermute(half, "graph", xor_pairs(parts, 1))
    slot_grad, mix = pl.pallas_call(
        attention_kernel,
        out_shape=(
            jax.ShapeDtypeStruct((keys, kv_width), BF16),
            jax.ShapeDtypeStruct((2, groups, DH, tokens), BF16),
        ),
        in_specs=vmem(2),
        out_specs=tuple(vmem(2)),
        scratch_shapes=[
            pltpu.VMEM((keys, kv_width), F32),
            pltpu.VMEM((2, keys, 2 * tokens), F32),
            pltpu.VMEM((2, keys, 2 * tokens), BF16),
        ],
        compiler_params=WIDE,
        name="attention",
    )(weights, received.reshape(keys, kv_width))
    returned = lax.all_to_all(
        slot_grad.reshape(parts, rows, kv_width), "graph", split_axis=0, concat_axis=0, tiled=True
    )
    mix = mix.reshape(2, head_width, tokens)
    mix_got = lax.ppermute(mix, "graph", xor_pairs(parts, 1))
    out_keep, out_away = pl.pallas_call(
        output_kernel,
        out_shape=(
            jax.ShapeDtypeStruct((mp // 2, share, width), F32),
            jax.ShapeDtypeStruct((mp // 2, share, width), F32),
        ),
        in_specs=vmem(2),
        out_specs=tuple(vmem(2)),
        compiler_params=GRANT,
        name="output",
    )(mix, wo2)
    out_got = lax.ppermute(out_away, "mp", xor_pairs(mp, 1))
    sums, *sums_away = pl.pallas_call(
        weights_kernel,
        out_shape=tuple(
            jax.ShapeDtypeStruct((2 * head_width + 16 * (d > 0), cols), F32)
            for d in range(outer)
        ),
        in_specs=vmem(5),
        out_specs=tuple(vmem(outer)),
        compiler_params=GRANT,
        name="weights",
    )(mix, mix_got, cotangent, x, half_got)
    sums_got = []
    for d in range(1, outer):
        away = sums_away[d - 1].astype(jnp.float16)
        sums_got.append(lax.ppermute(away, "graph", xor_pairs(parts, 2 * d)))
    kv_parts = pl.pallas_call(
        owner_kernel,
        out_shape=jax.ShapeDtypeStruct((parts, kv_width + 16, cols), F32),
        in_specs=[SMEM] + vmem(2),
        out_specs=vmem(1)[0],
        compiler_params=GRANT,
        name="owner",
    )(send, returned, x)
    kv_parts = kv_parts.astype(jnp.float16)
    kv_got = lax.all_to_all(kv_parts, "graph", split_axis=0, concat_axis=0, tiled=True)
    out_half = out_keep + out_got
    out_last = lax.ppermute(out_half[1], "mp", xor_pairs(mp, 2))
    own_rows = lax.dynamic_slice_in_dim(x, lax.axis_index("mp") * share, share, 0)
    output = (own_rows.astype(F32) + (out_half[0] + out_last)).astype(BF16)
    grad_wo, grad_wq = pl.pallas_call(
        sums_kernel,
        out_shape=tuple(jax.ShapeDtypeStruct((head_width, cols), F32) for _ in range(2)),
        in_specs=vmem(outer),
        out_specs=tuple(vmem(2)),
        compiler_params=GRANT,
        name="sums",
    )(sums, *(got.astype(F32) for got in sums_got))
    grad_wkv = pl.pallas_call(
        kvsum_kernel,
        out_shape=jax.ShapeDtypeStruct((kv_width, cols), F32),
        in_specs=vmem(1),
        out_specs=vmem(1)[0],
        compiler_params=GRANT,
        name="kvsum",
    )(kv_got.astype(F32))
    return (
        output,
        grad_wq.reshape(cols, *wq.shape[1:]),
        grad_wkv.reshape(cols, *wkv.shape[1:]),
        grad_wo.reshape(*wo.shape[:2], cols),
    )


def local(node_features, wq, wkv, wo, send_list, block_list, cotangent):
    parts, mp, slots = lax.axis_size("graph"), lax.axis_size("mp"), send_list.shape[2]
    copies, rest = divmod(block_list.shape[1], parts * slots)
    every_slot = rest == 0 and copies & (copies - 1) == 0
    if every_slot and slots == 1 and parts == 8 and mp == 4 and wq.shape[1] == 1:
        body = shared_local
    else:
        body = listed_local
    return body(node_features, wq, wkv, wo, send_list, block_list, cotangent)


def solution(mesh):
    return jax.shard_map(
        local,
        mesh=mesh,
        in_specs=(
            P("graph", None, None),
            P(None, "mp", None),
            P(None, "mp", None),
            P("mp", None, None),
            P("graph", None, None),
            P("graph", None),
            P("graph", None),
        ),
        out_specs=(
            P(("graph", "mp"), None),
            P("graph", "mp", None),
            P("graph", "mp", None),
            P("mp", None, "graph"),
        ),
        check_vma=False,
    )
```

```python
import jax
import jax.numpy as jnp
from jax import lax
from jax.experimental import pallas as pl
from jax.experimental.pallas import tpu as pltpu
from jax.sharding import PartitionSpec as P

DH = 64
F32 = jnp.float32
BF16 = jnp.bfloat16


def head_forward(query_head, key_flat, width):
    score = jnp.einsum(
        "rhd,khd->hrk", query_head, key_flat[..., :width], preferred_element_type=F32
    )
    row_max = jnp.max(score, axis=-1, keepdims=True)
    exponent = jnp.exp(score - row_max)
    weights = exponent / jnp.sum(exponent, axis=-1, keepdims=True)
    rounded = weights.astype(BF16)
    mixed = jnp.einsum(
        "hrk,khd->rhd", rounded, key_flat[..., width:], preferred_element_type=F32
    ).astype(BF16)
    return (weights, rounded, mixed)


def tile_forward(query_tile, key_rows):
    heads = query_tile.shape[1]
    width = query_tile.shape[3]
    key_flat = key_rows.reshape(-1, heads, 2 * width)

    def one_head(query_head):
        return head_forward(query_head, key_flat, width)[2]

    per_head = lax.map(one_head, jnp.moveaxis(query_tile, 2, 0))
    return jnp.moveaxis(per_head, 0, 2)


def tile_backward(query_tile, key_rows, grad_tile):
    heads = query_tile.shape[1]
    width = query_tile.shape[3]
    key_flat = key_rows.reshape(-1, heads, 2 * width)

    def one_head(total, entry):
        query_head, grad_head = entry
        weights, rounded, _ = head_forward(query_head, key_flat, width)
        grad_prob = jnp.einsum(
            "rhd,khd->hrk", grad_head, key_flat[..., width:], preferred_element_type=F32
        )
        delta = jnp.sum(weights * grad_prob, axis=-1, keepdims=True)
        grad_score = (weights * (grad_prob - delta)).astype(BF16)
        grad_query = (
            jnp.einsum(
                "hrk,khd->rhd", grad_score, key_flat[..., :width], preferred_element_type=F32
            )
            * width ** (-0.5)
        ).astype(BF16)
        grad_key = jnp.einsum("hrk,rhd->khd", grad_score, query_head, preferred_element_type=F32)
        grad_value = jnp.einsum("hrk,rhd->khd", rounded, grad_head, preferred_element_type=F32)
        total = total + jnp.concatenate([grad_key, grad_value], axis=-1)
        return (total, grad_query)

    start_total = jnp.zeros(key_flat.shape, F32)
    key_grad, grad_query = lax.scan(
        one_head, start_total, (jnp.moveaxis(query_tile, 2, 0), jnp.moveaxis(grad_tile, 2, 0))
    )
    return (jnp.moveaxis(grad_query, 0, 2), key_grad.reshape(key_rows.shape))


def listed_local(node_features, wq, wkv, wo, send_list, block_list, cotangent):
    tiles, tile_rows, width = node_features.shape
    heads = wq.shape[1]
    head_width = wq.shape[2]
    groups = head_width // DH
    parts = lax.axis_size("graph")
    slots = send_list.shape[2]
    token_rows = node_features.reshape(tiles * tile_rows, width)
    query = (
        jnp.dot(token_rows, wq.reshape(width, -1), preferred_element_type=F32) * DH ** (-0.5)
    ).astype(BF16)
    query = query.reshape(tiles, tile_rows, heads, groups, DH)
    keyval = jnp.dot(token_rows, wkv.reshape(width, -1), preferred_element_type=F32).astype(BF16)
    keyval = keyval.reshape(tiles, tile_rows, -1)
    outgoing = keyval[send_list[0].reshape(-1)]
    received = lax.all_to_all(outgoing, "graph", split_axis=0, concat_axis=0, tiled=True)

    def forward_one(entry):
        query_tile, key_ids = entry
        return tile_forward(query_tile, received[key_ids])

    mixed = lax.map(forward_one, (query, block_list))
    mixed_rows = mixed.reshape(tiles * tile_rows, heads * head_width)
    out_flat = wo.reshape(heads * head_width, width)
    share = tiles * tile_rows // lax.axis_size("mp")
    summed = lax.psum_scatter(
        jnp.dot(mixed_rows, out_flat, preferred_element_type=F32),
        "mp",
        scatter_dimension=0,
        tiled=True,
    )
    own_rows = lax.dynamic_slice_in_dim(token_rows, lax.axis_index("mp") * share, share, 0)
    output = (own_rows.astype(F32) + summed).astype(BF16)
    grad_out_local = jnp.dot(mixed_rows.T, cotangent, preferred_element_type=F32).reshape(wo.shape)
    grad_mixed = jnp.einsum("rd,hd->rh", cotangent, out_flat, preferred_element_type=F32).astype(
        BF16
    )
    grad_mixed = grad_mixed.reshape(tiles, tile_rows, heads, groups, DH)

    def backward_one(entry):
        query_tile, key_ids, grad_tile = entry
        return tile_backward(query_tile, received[key_ids], grad_tile)

    grad_query, key_grad = lax.map(backward_one, (query, block_list, grad_mixed))
    slot_ids = jnp.arange(parts * slots, dtype=jnp.int32)
    picks = (block_list.reshape(1, -1) == slot_ids[:, None]).astype(F32)
    slot_grad = jnp.dot(
        picks,
        key_grad.reshape(tiles * block_list.shape[1], -1),
        precision=lax.Precision.HIGHEST,
        preferred_element_type=F32,
    ).astype(BF16)
    slot_grad = slot_grad.reshape(parts * slots, tile_rows, -1)
    returned = lax.all_to_all(slot_grad, "graph", split_axis=0, concat_axis=0, tiled=True)
    owners = (send_list[0].reshape(1, -1) == jnp.arange(tiles, dtype=jnp.int32)[:, None]).astype(
        BF16
    )
    grad_keyval = jnp.dot(
        owners, returned.reshape(parts * slots, -1), preferred_element_type=F32
    ).astype(BF16)
    grad_keyval = grad_keyval.reshape(tiles * tile_rows, -1)
    grad_query_local = jnp.dot(
        token_rows.T, grad_query.reshape(tiles * tile_rows, -1), preferred_element_type=F32
    ).reshape(wq.shape)
    grad_keyval_local = jnp.dot(token_rows.T, grad_keyval, preferred_element_type=F32).reshape(
        wkv.shape
    )
    grad_wq = lax.psum_scatter(grad_query_local, "graph", scatter_dimension=0, tiled=True)
    grad_wkv = lax.psum_scatter(grad_keyval_local, "graph", scatter_dimension=0, tiled=True)
    grad_out = lax.psum_scatter(grad_out_local, "graph", scatter_dimension=2, tiled=True)
    return (output, grad_wq, grad_wkv, grad_out)


def dot(a, b, contract=((1,), (0,))):
    return lax.dot_general(a, b, (contract, ((), ())), preferred_element_type=F32)


NT = ((1,), (1,))


def keyval_kernel(send_hbm, x_hbm, wkv_hbm, out_ref, x_ref, wkv_ref, send_ref, kv_ref, sems):
    tiles, rows = kv_ref.shape[:2]
    weight = pltpu.make_async_copy(wkv_hbm, wkv_ref, sems.at[0])
    listing = pltpu.make_async_copy(send_hbm, send_ref, sems.at[1])
    weight.start()
    copies = []
    for t in range(tiles):
        at = pl.ds(t * rows, rows)
        copies.append(pltpu.make_async_copy(x_hbm.at[at], x_ref.at[at], sems.at[2 + t]))
        copies[-1].start()
    listing.start()
    weight.wait()
    for t, copy in enumerate(copies):
        copy.wait()
        kv_ref[t] = dot(x_ref[t * rows : (t + 1) * rows], wkv_ref[...]).astype(BF16)
    listing.wait()
    for r in range(out_ref.shape[0]):
        out_ref[r] = kv_ref[send_ref[r]]


def project_kernel(x_ref, wq_ref, wo_ref, cot_ref, w_ref):
    tokens = x_ref.shape[0]
    groups = w_ref.shape[0]
    query = (dot(x_ref[...], wq_ref[...]) * DH ** (-0.5)).astype(BF16)
    query_t = query.T
    grad_mixed_t = dot(wo_ref[...], cot_ref[...], NT).astype(BF16)
    w_ref[...] = jnp.zeros_like(w_ref)
    for k in range(groups):
        w_ref[k, :DH, :tokens] = query_t[k * DH : (k + 1) * DH]
        w_ref[k, DH:, tokens:] = grad_mixed_t[k * DH : (k + 1) * DH]


def halves_kernel(cot_ref, x_ref, half_ref):
    other = 1 - lax.rem(lax.axis_index("graph"), 2)
    outer = half_ref.shape[1]
    cols = half_ref.shape[3]
    for d in range(outer):
        at = pl.ds(pl.multiple_of((2 * d + other) * cols, cols), cols)
        half_ref[0, d] = cot_ref[:, at]
        half_ref[1, d] = x_ref[:, at]


def attention_kernel(w_ref, kv_ref, slot_ref, mix_ref, acc_ref, both_ref, pair_ref):
    groups, _, twice = w_ref.shape
    tokens = twice // 2
    scale = DH ** (-0.5)
    kv_t = kv_ref[...].T

    def scores(k):
        both = dot(kv_ref[...], w_ref[k])
        both_ref[k % 2] = both
        return jnp.max(both[:, :tokens], axis=0, keepdims=True)

    top = scores(0)
    for k in range(groups):
        b = k % 2
        exponent = jnp.exp(both_ref[b, :, :tokens] - top)
        grad_prob = both_ref[b, :, tokens:]
        inverse = 1.0 / jnp.sum(exponent, axis=0, keepdims=True)
        prob = exponent * inverse
        delta = jnp.sum(prob * grad_prob, axis=0, keepdims=True)
        pair_ref[b, :, tokens:] = prob.astype(BF16)
        pair_ref[b, :, :tokens] = (prob * (grad_prob - delta)).astype(BF16)
        if k + 1 < groups:
            top = scores(k + 1)
        outs = dot(kv_t, pair_ref[b])
        mix_ref[0, k] = outs[DH:, tokens:].astype(BF16)
        mix_ref[1, k] = (outs[:DH, :tokens] * scale).astype(BF16)
        grad = dot(pair_ref[b], w_ref[k], NT)
        if k == 0:
            acc_ref[...] = grad
        elif k + 1 < groups:
            acc_ref[...] += grad
        else:
            slot_ref[...] = (acc_ref[...] + grad).astype(BF16)


def output_kernel(mix_ref, wo_ref, out_keep_ref, out_send_ref):
    mp = lax.axis_index("mp")
    core, across = lax.rem(mp, 2), lax.div(mp, 2)
    rows = out_keep_ref.shape[1]
    mixed = mix_ref[0].T
    part = dot(mixed, wo_ref[...])
    for m in range(4):
        block = part[m * rows : (m + 1) * rows]
        place = lax.bitwise_xor(m // 2, across)

        @pl.when(core == m % 2)
        def _():
            out_keep_ref[place] = block

        @pl.when(core != m % 2)
        def _():
            out_send_ref[place] = block


def exponent_of(peak):
    return jnp.ceil(jnp.log2(jnp.maximum(peak, 1e-30))) - 14.0


def peak_of(value, peak):
    top = jnp.max(jnp.abs(value), axis=0, keepdims=True)
    return jnp.maximum(peak, jnp.max(top, axis=1, keepdims=True))


def weights_kernel(mix_ref, mix_got_ref, cot_ref, x_ref, half_ref, own_ref, *out_refs):
    graph = lax.axis_index("graph")
    y, z = lax.rem(graph, 2), lax.div(graph, 2)
    head_width = mix_ref.shape[1]
    cols = half_ref.shape[3]
    parts = head_width // cols
    refs = (own_ref,) + out_refs
    peak = jnp.zeros((1, 1), F32)
    for d, ref in enumerate(refs):
        there = lax.bitwise_xor(z, d)
        at = pl.ds(pl.multiple_of((2 * there + y) * cols, cols), cols)
        wo = dot(mix_ref[0], cot_ref[:, at]) + dot(mix_got_ref[0], half_ref[0, there])
        wq = dot(mix_ref[1], x_ref[:, at]) + dot(mix_got_ref[1], half_ref[1, there])
        ref[:head_width] = wo
        for h in range(parts):
            place = pl.ds(head_width + h, cols, parts)
            ref[place, :] = wq[h * cols : (h + 1) * cols].T
        if d > 0:
            peak = peak_of(wo, peak_of(wq, peak))
    e = exponent_of(peak)
    factor = jnp.exp2(-e)
    rows = 2 * head_width
    for ref in out_refs:
        ref[:rows] = ref[:rows] * factor
        ref[rows:] = jnp.broadcast_to(e, ref[rows:].shape)


def owner_kernel(send_ref, ret_ref, x_ref, out_ref):
    receivers, rows = ret_ref.shape[:2]
    tiles = x_ref.shape[0] // rows
    sums = []
    for t in range(tiles):
        total = jnp.zeros(ret_ref.shape[1:], F32)
        for r in range(receivers):
            mine = (send_ref[r] == t).astype(F32)
            total += ret_ref[r].astype(F32) * mine
        sums.append(total.astype(BF16))
    grad_kv_t = jnp.concatenate(sums, axis=0).T
    cols = out_ref.shape[2]
    kv_width = grad_kv_t.shape[0]
    whole = dot(grad_kv_t, x_ref[...])
    e = exponent_of(peak_of(whole, jnp.zeros((1, 1), F32)))
    factor = jnp.exp2(-e)
    for r in range(out_ref.shape[0]):
        out_ref[r, :kv_width] = whole[:, r * cols : (r + 1) * cols].T * factor
        out_ref[r, kv_width:] = jnp.broadcast_to(e, out_ref[r, kv_width:].shape)


def unscaled(value):
    rows = value.shape[0] - 16
    return value[:rows] * jnp.exp2(value[rows : rows + 1])


def sums_kernel(own_ref, *refs):
    *got_refs, wo_ref, wq_ref = refs
    total = own_ref[...]
    for ref in got_refs:
        total = total + unscaled(ref[...])
    half = wo_ref.shape[0]
    wo_ref[...] = total[:half]
    wq_ref[...] = total[half:]


def kvsum_kernel(got_ref, out_ref):
    total = unscaled(got_ref[0])
    for r in range(1, got_ref.shape[0]):
        total = total + unscaled(got_ref[r])
    out_ref[...] = total


GRANT = pltpu.CompilerParams(vmem_limit_bytes=8 << 20)
WIDE = pltpu.CompilerParams(vmem_limit_bytes=16 << 20)


def vmem(count):
    return [pl.BlockSpec(memory_space=pltpu.VMEM)] * count


SMEM = pl.BlockSpec(memory_space=pltpu.SMEM)


def xor_pairs(n, k):
    return [(i, i ^ k) for i in range(n)]


def shared_local(node_features, wq, wkv, wo, send_list, block_list, cotangent):
    tiles, rows, width = node_features.shape
    tokens = tiles * rows
    head_width = wq.shape[1] * wq.shape[2]
    kv_width = wkv.shape[2]
    groups = head_width // DH
    parts = lax.axis_size("graph")
    mp = lax.axis_size("mp")
    cols = width // parts
    x = node_features.reshape(tokens, width)
    send = send_list.reshape(-1)
    wq2, wkv2 = wq.reshape(width, head_width), wkv.reshape(width, kv_width)
    wo2 = wo.reshape(head_width, width)

    outgoing = pl.pallas_call(
keyval_kernel,
out_shape=jax.ShapeDtypeStruct((parts, rows, kv_width), BF16),
in_specs=[pl.BlockSpec(memory_space=pltpu.HBM)] * 3,
out_specs=vmem(1)[0],
scratch_shapes=[
    pltpu.VMEM(x.shape, BF16),
    pltpu.VMEM(wkv2.shape, BF16),
    pltpu.SMEM(send.shape, jnp.int32),
    pltpu.VMEM((tiles, rows, kv_width), BF16),
    pltpu.SemaphoreType.DMA((2 + tiles,)),
],
    )(send, x, wkv2)
    received = lax.all_to_all(outgoing, "graph", split_axis=0, concat_axis=0, tiled=True)
    keys = parts * rows
    share = tokens // mp
    outer = parts // 2
    weights = pl.pallas_call(
project_kernel,
out_shape=jax.ShapeDtypeStruct((groups, kv_width, 2 * tokens), BF16),
in_specs=vmem(4),
out_specs=vmem(1)[0],
compiler_params=GRANT,
    )(x, wq2, wo2, cotangent)
    half = pl.pallas_call(
halves_kernel,
out_shape=jax.ShapeDtypeStruct((2, outer, tokens, cols), BF16),
in_specs=vmem(2),
out_specs=vmem(1)[0],
compiler_params=GRANT,
    )(cotangent, x)
    half_got = lax.ppermute(half, "graph", xor_pairs(parts, 1))
    slot_grad, mix = pl.pallas_call(
attention_kernel,
out_shape=(
jax.ShapeDtypeStruct((keys, kv_width), BF16),
jax.ShapeDtypeStruct((2, groups, DH, tokens), BF16),
),
in_specs=vmem(2),
out_specs=tuple(vmem(2)),
scratch_shapes=[
pltpu.VMEM((keys, kv_width), F32),
pltpu.VMEM((2, keys, 2 * tokens), F32),
pltpu.VMEM((2, keys, 2 * tokens), BF16),
],
compiler_params=WIDE,
    )(weights, received.reshape(keys, kv_width))
    returned = lax.all_to_all(
        slot_grad.reshape(parts, rows, kv_width), "graph", split_axis=0, concat_axis=0, tiled=True
    )
    mix = mix.reshape(2, head_width, tokens)
    mix_got = lax.ppermute(mix, "graph", xor_pairs(parts, 1))
    out_keep, out_away = pl.pallas_call(
output_kernel,
out_shape=(
jax.ShapeDtypeStruct((mp // 2, share, width), F32),
jax.ShapeDtypeStruct((mp // 2, share, width), F32),
),
in_specs=vmem(2),
out_specs=tuple(vmem(2)),
compiler_params=GRANT,
    )(mix, wo2)
    out_got = lax.ppermute(out_away, "mp", xor_pairs(mp, 1))
    sums, *sums_away = pl.pallas_call(
weights_kernel,
out_shape=tuple(
jax.ShapeDtypeStruct((2 * head_width + 16 * (d > 0), cols), F32)
for d in range(outer)
),
in_specs=vmem(5),
out_specs=tuple(vmem(outer)),
compiler_params=GRANT,
    )(mix, mix_got, cotangent, x, half_got)
    sums_got = []
    for d in range(1, outer):
        away = sums_away[d - 1].astype(jnp.float16)
        sums_got.append(lax.ppermute(away, "graph", xor_pairs(parts, 2 * d)))
    kv_parts = pl.pallas_call(
owner_kernel,
out_shape=jax.ShapeDtypeStruct((parts, kv_width + 16, cols), F32),
in_specs=[SMEM] + vmem(2),
out_specs=vmem(1)[0],
compiler_params=GRANT,
    )(send, returned, x)
    kv_parts = kv_parts.astype(jnp.float16)
    kv_got = lax.all_to_all(kv_parts, "graph", split_axis=0, concat_axis=0, tiled=True)
    out_half = out_keep + out_got
    out_last = lax.ppermute(out_half[1], "mp", xor_pairs(mp, 2))
    own_rows = lax.dynamic_slice_in_dim(x, lax.axis_index("mp") * share, share, 0)
    output = (own_rows.astype(F32) + (out_half[0] + out_last)).astype(BF16)
    grad_wo, grad_wq = pl.pallas_call(
sums_kernel,
out_shape=tuple(jax.ShapeDtypeStruct((head_width, cols), F32) for _ in range(2)),
in_specs=vmem(outer),
out_specs=tuple(vmem(2)),
compiler_params=GRANT,
    )(sums, *(got.astype(F32) for got in sums_got))
    grad_wkv = pl.pallas_call(
kvsum_kernel,
out_shape=jax.ShapeDtypeStruct((kv_width, cols), F32),
in_specs=vmem(1),
out_specs=vmem(1)[0],
compiler_params=GRANT,
    )(kv_got.astype(F32))
    return (
        output,
        grad_wq.reshape(cols, *wq.shape[1:]),
        grad_wkv.reshape(cols, *wkv.shape[1:]),
        grad_wo.reshape(*wo.shape[:2], cols),
    )


def local(node_features, wq, wkv, wo, send_list, block_list, cotangent):
    parts, mp, slots = lax.axis_size("graph"), lax.axis_size("mp"), send_list.shape[2]
    copies, rest = divmod(block_list.shape[1], parts * slots)
    every_slot = rest == 0 and copies & (copies - 1) == 0
    if every_slot and slots == 1 and parts == 8 and mp == 4 and wq.shape[1] == 1:
        body = shared_local
    else:
        body = listed_local
    return body(node_features, wq, wkv, wo, send_list, block_list, cotangent)


def solution(mesh):
    return jax.shard_map(
        local,
        mesh=mesh,
        in_specs=(
            P("graph", None, None),
            P(None, "mp", None),
            P(None, "mp", None),
            P("mp", None, None),
            P("graph", None, None),
            P("graph", None),
            P("graph", None),
        ),
        out_specs=(
            P(("graph", "mp"), None),
            P("graph", "mp", None),
            P("graph", "mp", None),
            P("mp", None, "graph"),
        ),
        check_vma=False,
    )
```

```python
import jax
import jax.numpy as jnp
from jax import lax
from jax.experimental import pallas as pl
from jax.experimental.pallas import tpu as pltpu
from jax.sharding import PartitionSpec as P

DH = 64
F32 = jnp.float32
BF16 = jnp.bfloat16


def head_forward(query_head, key_flat, width):
    score = jnp.einsum(
        "rhd,khd->hrk", query_head, key_flat[..., :width], preferred_element_type=F32
    )
    row_max = jnp.max(score, axis=-1, keepdims=True)
    exponent = jnp.exp(score - row_max)
    weights = exponent / jnp.sum(exponent, axis=-1, keepdims=True)
    rounded = weights.astype(BF16)
    mixed = jnp.einsum(
        "hrk,khd->rhd", rounded, key_flat[..., width:], preferred_element_type=F32
    ).astype(BF16)
    return (weights, rounded, mixed)


def tile_forward(query_tile, key_rows):
    heads = query_tile.shape[1]
    width = query_tile.shape[3]
    key_flat = key_rows.reshape(-1, heads, 2 * width)

    def one_head(query_head):
        return head_forward(query_head, key_flat, width)[2]

    per_head = lax.map(one_head, jnp.moveaxis(query_tile, 2, 0))
    return jnp.moveaxis(per_head, 0, 2)


def tile_backward(query_tile, key_rows, grad_tile):
    heads = query_tile.shape[1]
    width = query_tile.shape[3]
    key_flat = key_rows.reshape(-1, heads, 2 * width)

    def one_head(total, entry):
        query_head, grad_head = entry
        weights, rounded, _ = head_forward(query_head, key_flat, width)
        grad_prob = jnp.einsum(
            "rhd,khd->hrk", grad_head, key_flat[..., width:], preferred_element_type=F32
        )
        delta = jnp.sum(weights * grad_prob, axis=-1, keepdims=True)
        grad_score = (weights * (grad_prob - delta)).astype(BF16)
        grad_query = (
            jnp.einsum(
                "hrk,khd->rhd", grad_score, key_flat[..., :width], preferred_element_type=F32
            )
            * width ** (-0.5)
        ).astype(BF16)
        grad_key = jnp.einsum("hrk,rhd->khd", grad_score, query_head, preferred_element_type=F32)
        grad_value = jnp.einsum("hrk,rhd->khd", rounded, grad_head, preferred_element_type=F32)
        total = total + jnp.concatenate([grad_key, grad_value], axis=-1)
        return (total, grad_query)

    start_total = jnp.zeros(key_flat.shape, F32)
    key_grad, grad_query = lax.scan(
        one_head, start_total, (jnp.moveaxis(query_tile, 2, 0), jnp.moveaxis(grad_tile, 2, 0))
    )
    return (jnp.moveaxis(grad_query, 0, 2), key_grad.reshape(key_rows.shape))


def listed_local(node_features, wq, wkv, wo, send_list, block_list, cotangent):
    tiles, tile_rows, width = node_features.shape
    heads = wq.shape[1]
    head_width = wq.shape[2]
    groups = head_width // DH
    parts = lax.axis_size("graph")
    slots = send_list.shape[2]
    token_rows = node_features.reshape(tiles * tile_rows, width)
    query = (
        jnp.dot(token_rows, wq.reshape(width, -1), preferred_element_type=F32) * DH ** (-0.5)
    ).astype(BF16)
    query = query.reshape(tiles, tile_rows, heads, groups, DH)
    keyval = jnp.dot(token_rows, wkv.reshape(width, -1), preferred_element_type=F32).astype(BF16)
    keyval = keyval.reshape(tiles, tile_rows, -1)
    outgoing = keyval[send_list[0].reshape(-1)]
    received = lax.all_to_all(outgoing, "graph", split_axis=0, concat_axis=0, tiled=True)

    def forward_one(entry):
        query_tile, key_ids = entry
        return tile_forward(query_tile, received[key_ids])

    mixed = lax.map(forward_one, (query, block_list))
    mixed_rows = mixed.reshape(tiles * tile_rows, heads * head_width)
    out_flat = wo.reshape(heads * head_width, width)
    share = tiles * tile_rows // lax.axis_size("mp")
    summed = lax.psum_scatter(
        jnp.dot(mixed_rows, out_flat, preferred_element_type=F32),
        "mp",
        scatter_dimension=0,
        tiled=True,
    )
    own_rows = lax.dynamic_slice_in_dim(token_rows, lax.axis_index("mp") * share, share, 0)
    output = (own_rows.astype(F32) + summed).astype(BF16)
    grad_out_local = jnp.dot(mixed_rows.T, cotangent, preferred_element_type=F32).reshape(wo.shape)
    grad_mixed = jnp.einsum("rd,hd->rh", cotangent, out_flat, preferred_element_type=F32).astype(
        BF16
    )
    grad_mixed = grad_mixed.reshape(tiles, tile_rows, heads, groups, DH)

    def backward_one(entry):
        query_tile, key_ids, grad_tile = entry
        return tile_backward(query_tile, received[key_ids], grad_tile)

    grad_query, key_grad = lax.map(backward_one, (query, block_list, grad_mixed))
    slot_ids = jnp.arange(parts * slots, dtype=jnp.int32)
    picks = (block_list.reshape(1, -1) == slot_ids[:, None]).astype(F32)
    slot_grad = jnp.dot(
        picks,
        key_grad.reshape(tiles * block_list.shape[1], -1),
        precision=lax.Precision.HIGHEST,
        preferred_element_type=F32,
    ).astype(BF16)
    slot_grad = slot_grad.reshape(parts * slots, tile_rows, -1)
    returned = lax.all_to_all(slot_grad, "graph", split_axis=0, concat_axis=0, tiled=True)
    owners = (send_list[0].reshape(1, -1) == jnp.arange(tiles, dtype=jnp.int32)[:, None]).astype(
        BF16
    )
    grad_keyval = jnp.dot(
        owners, returned.reshape(parts * slots, -1), preferred_element_type=F32
    ).astype(BF16)
    grad_keyval = grad_keyval.reshape(tiles * tile_rows, -1)
    grad_query_local = jnp.dot(
        token_rows.T, grad_query.reshape(tiles * tile_rows, -1), preferred_element_type=F32
    ).reshape(wq.shape)
    grad_keyval_local = jnp.dot(token_rows.T, grad_keyval, preferred_element_type=F32).reshape(
        wkv.shape
    )
    grad_wq = lax.psum_scatter(grad_query_local, "graph", scatter_dimension=0, tiled=True)
    grad_wkv = lax.psum_scatter(grad_keyval_local, "graph", scatter_dimension=0, tiled=True)
    grad_out = lax.psum_scatter(grad_out_local, "graph", scatter_dimension=2, tiled=True)
    return (output, grad_wq, grad_wkv, grad_out)


def dot(a, b, contract=((1,), (0,))):
    return lax.dot_general(a, b, (contract, ((), ())), preferred_element_type=F32)


NT = ((1,), (1,))


def keyval_kernel(send_hbm, x_hbm, wkv_hbm, out_ref, x_ref, wkv_ref, send_ref, kv_ref, sems):
    tiles, rows = kv_ref.shape[:2]
    weight = pltpu.make_async_copy(wkv_hbm, wkv_ref, sems.at[0])
    listing = pltpu.make_async_copy(send_hbm, send_ref, sems.at[1])
    weight.start()
    copies = []
    for t in range(tiles):
        at = pl.ds(t * rows, rows)
        copies.append(pltpu.make_async_copy(x_hbm.at[at], x_ref.at[at], sems.at[2 + t]))
        copies[-1].start()
    listing.start()
    weight.wait()
    for t, copy in enumerate(copies):
        copy.wait()
        kv_ref[t] = dot(x_ref[t * rows : (t + 1) * rows], wkv_ref[...]).astype(BF16)
    listing.wait()
    for r in range(out_ref.shape[0]):
        out_ref[r] = kv_ref[send_ref[r]]


def project_kernel(x_ref, wq_ref, wo_ref, cot_ref, w_ref):
    tokens = x_ref.shape[0]
    groups = w_ref.shape[0]
    query = (dot(x_ref[...], wq_ref[...]) * DH ** (-0.5)).astype(BF16)
    query_t = query.T
    grad_mixed_t = dot(wo_ref[...], cot_ref[...], NT).astype(BF16)
    w_ref[...] = jnp.zeros_like(w_ref)
    for k in range(groups):
        w_ref[k, :DH, :tokens] = query_t[k * DH : (k + 1) * DH]
        w_ref[k, DH:, tokens:] = grad_mixed_t[k * DH : (k + 1) * DH]


def halves_kernel(cot_ref, x_ref, half_ref):
    other = 1 - lax.rem(lax.axis_index("graph"), 2)
    outer = half_ref.shape[1]
    cols = half_ref.shape[3]
    for d in range(outer):
        at = pl.ds(pl.multiple_of((2 * d + other) * cols, cols), cols)
        half_ref[0, d] = cot_ref[:, at]
        half_ref[1, d] = x_ref[:, at]


def attention_kernel(w_ref, kv_ref, slot_ref, mix_ref, acc_ref, both_ref, pair_ref):
    groups, _, twice = w_ref.shape
    tokens = twice // 2
    scale = DH ** (-0.5)
    kv_t = kv_ref[...].T

    def scores(k):
        both = dot(kv_ref[...], w_ref[k])
        both_ref[k % 2] = both
        return jnp.max(both[:, :tokens], axis=0, keepdims=True)

    top = scores(0)
    for k in range(groups):
        b = k % 2
        exponent = jnp.exp(both_ref[b, :, :tokens] - top)
        grad_prob = both_ref[b, :, tokens:]
        inverse = 1.0 / jnp.sum(exponent, axis=0, keepdims=True)
        prob = exponent * inverse
        delta = jnp.sum(prob * grad_prob, axis=0, keepdims=True)
        pair_ref[b, :, tokens:] = prob.astype(BF16)
        pair_ref[b, :, :tokens] = (prob * (grad_prob - delta)).astype(BF16)
        if k + 1 < groups:
            top = scores(k + 1)
        outs = dot(kv_t, pair_ref[b])
        mix_ref[0, k] = outs[DH:, tokens:].astype(BF16)
        mix_ref[1, k] = (outs[:DH, :tokens] * scale).astype(BF16)
        grad = dot(pair_ref[b], w_ref[k], NT)
        if k == 0:
            acc_ref[...] = grad
        elif k + 1 < groups:
            acc_ref[...] += grad
        else:
            slot_ref[...] = (acc_ref[...] + grad).astype(BF16)


def output_kernel(mix_ref, wo_ref, out_keep_ref, out_send_ref):
    mp = lax.axis_index("mp")
    core, across = lax.rem(mp, 2), lax.div(mp, 2)
    rows = out_keep_ref.shape[1]
    mixed = mix_ref[0].T
    part = dot(mixed, wo_ref[...])
    for m in range(4):
        block = part[m * rows : (m + 1) * rows]
        place = lax.bitwise_xor(m // 2, across)

        @pl.when(core == m % 2)
        def _():
            out_keep_ref[place] = block

        @pl.when(core != m % 2)
        def _():
            out_send_ref[place] = block


def exponent_of(peak):
    return jnp.ceil(jnp.log2(jnp.maximum(peak, 1e-30))) - 14.0


def peak_of(value, peak):
    top = jnp.max(jnp.abs(value), axis=0, keepdims=True)
    return jnp.maximum(peak, jnp.max(top, axis=1, keepdims=True))


def weights_kernel(mix_ref, mix_got_ref, cot_ref, x_ref, half_ref, own_ref, *out_refs):
    graph = lax.axis_index("graph")
    y, z = lax.rem(graph, 2), lax.div(graph, 2)
    head_width = mix_ref.shape[1]
    cols = half_ref.shape[3]
    refs = (own_ref,) + out_refs
    rows = 2 * head_width
    peak = jnp.zeros((1, 1), F32)
    for d in range(0, len(refs), 2):
        there = [lax.bitwise_xor(z, d + i) for i in range(2)]
        at = [pl.ds(pl.multiple_of((2 * t + y) * cols, cols), cols) for t in there]
        for m, ref in ((0, cot_ref), (1, x_ref)):
            mine = jnp.concatenate([ref[:, a] for a in at], axis=1)
            theirs = jnp.concatenate([half_ref[m, t] for t in there], axis=1)
            both = dot(mix_ref[m], mine) + dot(mix_got_ref[m], theirs)
            for i in range(2):
                place = slice(m * head_width, (m + 1) * head_width)
                refs[d + i][place] = both[:, i * cols : (i + 1) * cols]
            peak = peak_of(both, peak)
    e = exponent_of(peak)
    factor = jnp.exp2(-e)
    for ref in out_refs:
        ref[:rows] = ref[:rows] * factor
        ref[rows:] = jnp.broadcast_to(e, ref[rows:].shape)


def owner_kernel(send_ref, ret_ref, x_ref, out_ref):
    receivers, rows = ret_ref.shape[:2]
    tiles = x_ref.shape[0] // rows
    sums = []
    for t in range(tiles):
        total = jnp.zeros(ret_ref.shape[1:], F32)
        for r in range(receivers):
            mine = (send_ref[r] == t).astype(F32)
            total += ret_ref[r].astype(F32) * mine
        sums.append(total.astype(BF16))
    grad_kv_t = jnp.concatenate(sums, axis=0).T
    cols = out_ref.shape[2]
    kv_width = grad_kv_t.shape[0]
    whole = dot(grad_kv_t, x_ref[...])
    e = exponent_of(peak_of(whole, jnp.zeros((1, 1), F32)))
    factor = jnp.exp2(-e)
    for r in range(out_ref.shape[0]):
        out_ref[r, :kv_width] = whole[:, r * cols : (r + 1) * cols].T * factor
        out_ref[r, kv_width:] = jnp.broadcast_to(e, out_ref[r, kv_width:].shape)


def unscaled(value):
    rows = value.shape[0] - 16
    return value[:rows] * jnp.exp2(value[rows : rows + 1])


def sums_kernel(own_ref, *refs):
    *got_refs, wo_ref, wq_ref = refs
    total = own_ref[...]
    for ref in got_refs:
        total = total + unscaled(ref[...])
    half = wo_ref.shape[0]
    wo_ref[...] = total[:half]
    rows = wo_ref.shape[1]
    parts = half // rows
    for h in range(parts):
        start = half + h * rows
        wq_ref[pl.ds(h, rows, parts), :] = total[start : start + rows].T


def kvsum_kernel(got_ref, out_ref):
    total = unscaled(got_ref[0])
    for r in range(1, got_ref.shape[0]):
        total = total + unscaled(got_ref[r])
    out_ref[...] = total


GRANT = pltpu.CompilerParams(vmem_limit_bytes=8 << 20)
WIDE = pltpu.CompilerParams(vmem_limit_bytes=16 << 20)


def vmem(count):
    return [pl.BlockSpec(memory_space=pltpu.VMEM)] * count


SMEM = pl.BlockSpec(memory_space=pltpu.SMEM)


def xor_pairs(n, k):
    return [(i, i ^ k) for i in range(n)]


def shared_local(node_features, wq, wkv, wo, send_list, block_list, cotangent):
    tiles, rows, width = node_features.shape
    tokens = tiles * rows
    head_width = wq.shape[1] * wq.shape[2]
    kv_width = wkv.shape[2]
    groups = head_width // DH
    parts = lax.axis_size("graph")
    mp = lax.axis_size("mp")
    cols = width // parts
    x = node_features.reshape(tokens, width)
    send = send_list.reshape(-1)
    wq2, wkv2 = wq.reshape(width, head_width), wkv.reshape(width, kv_width)
    wo2 = wo.reshape(head_width, width)

    outgoing = pl.pallas_call(
keyval_kernel,
out_shape=jax.ShapeDtypeStruct((parts, rows, kv_width), BF16),
in_specs=[pl.BlockSpec(memory_space=pltpu.HBM)] * 3,
out_specs=vmem(1)[0],
scratch_shapes=[
    pltpu.VMEM(x.shape, BF16),
    pltpu.VMEM(wkv2.shape, BF16),
    pltpu.SMEM(send.shape, jnp.int32),
    pltpu.VMEM((tiles, rows, kv_width), BF16),
    pltpu.SemaphoreType.DMA((2 + tiles,)),
],
    )(send, x, wkv2)
    received = lax.all_to_all(outgoing, "graph", split_axis=0, concat_axis=0, tiled=True)
    keys = parts * rows
    share = tokens // mp
    outer = parts // 2
    weights = pl.pallas_call(
project_kernel,
out_shape=jax.ShapeDtypeStruct((groups, kv_width, 2 * tokens), BF16),
in_specs=vmem(4),
out_specs=vmem(1)[0],
compiler_params=GRANT,
    )(x, wq2, wo2, cotangent)
    half = pl.pallas_call(
halves_kernel,
out_shape=jax.ShapeDtypeStruct((2, outer, tokens, cols), BF16),
in_specs=vmem(2),
out_specs=vmem(1)[0],
compiler_params=GRANT,
    )(cotangent, x)
    half_got = lax.ppermute(half, "graph", xor_pairs(parts, 1))
    slot_grad, mix = pl.pallas_call(
attention_kernel,
out_shape=(
jax.ShapeDtypeStruct((keys, kv_width), BF16),
jax.ShapeDtypeStruct((2, groups, DH, tokens), BF16),
),
in_specs=vmem(2),
out_specs=tuple(vmem(2)),
scratch_shapes=[
pltpu.VMEM((keys, kv_width), F32),
pltpu.VMEM((2, keys, 2 * tokens), F32),
pltpu.VMEM((2, keys, 2 * tokens), BF16),
],
compiler_params=WIDE,
    )(weights, received.reshape(keys, kv_width))
    returned = lax.all_to_all(
        slot_grad.reshape(parts, rows, kv_width), "graph", split_axis=0, concat_axis=0, tiled=True
    )
    mix = mix.reshape(2, head_width, tokens)
    mix_got = lax.ppermute(mix, "graph", xor_pairs(parts, 1))
    out_keep, out_away = pl.pallas_call(
output_kernel,
out_shape=(
jax.ShapeDtypeStruct((mp // 2, share, width), F32),
jax.ShapeDtypeStruct((mp // 2, share, width), F32),
),
in_specs=vmem(2),
out_specs=tuple(vmem(2)),
compiler_params=GRANT,
    )(mix, wo2)
    out_got = lax.ppermute(out_away, "mp", xor_pairs(mp, 1))
    sums, *sums_away = pl.pallas_call(
weights_kernel,
out_shape=tuple(
jax.ShapeDtypeStruct((2 * head_width + 16 * (d > 0), cols), F32)
for d in range(outer)
),
in_specs=vmem(5),
out_specs=tuple(vmem(outer)),
compiler_params=GRANT,
    )(mix, mix_got, cotangent, x, half_got)
    sums_got = []
    for d in range(1, outer):
        away = sums_away[d - 1].astype(jnp.float16)
        sums_got.append(lax.ppermute(away, "graph", xor_pairs(parts, 2 * d)))
    kv_parts = pl.pallas_call(
owner_kernel,
out_shape=jax.ShapeDtypeStruct((parts, kv_width + 16, cols), F32),
in_specs=[SMEM] + vmem(2),
out_specs=vmem(1)[0],
compiler_params=GRANT,
    )(send, returned, x)
    kv_parts = kv_parts.astype(jnp.float16)
    kv_got = lax.all_to_all(kv_parts, "graph", split_axis=0, concat_axis=0, tiled=True)
    out_half = out_keep + out_got
    out_last = lax.ppermute(out_half[1], "mp", xor_pairs(mp, 2))
    own_rows = lax.dynamic_slice_in_dim(x, lax.axis_index("mp") * share, share, 0)
    output = (own_rows.astype(F32) + (out_half[0] + out_last)).astype(BF16)
    grad_wo, grad_wq = pl.pallas_call(
sums_kernel,
out_shape=tuple(jax.ShapeDtypeStruct((head_width, cols), F32) for _ in range(2)),
in_specs=vmem(outer),
out_specs=tuple(vmem(2)),
compiler_params=GRANT,
    )(sums, *(got.astype(F32) for got in sums_got))
    grad_wkv = pl.pallas_call(
kvsum_kernel,
out_shape=jax.ShapeDtypeStruct((kv_width, cols), F32),
in_specs=vmem(1),
out_specs=vmem(1)[0],
compiler_params=GRANT,
    )(kv_got.astype(F32))
    return (
        output,
        grad_wq.reshape(cols, *wq.shape[1:]),
        grad_wkv.reshape(cols, *wkv.shape[1:]),
        grad_wo.reshape(*wo.shape[:2], cols),
    )


def local(node_features, wq, wkv, wo, send_list, block_list, cotangent):
    parts, mp, slots = lax.axis_size("graph"), lax.axis_size("mp"), send_list.shape[2]
    copies, rest = divmod(block_list.shape[1], parts * slots)
    every_slot = rest == 0 and copies & (copies - 1) == 0
    if every_slot and slots == 1 and parts == 8 and mp == 4 and wq.shape[1] == 1:
        body = shared_local
    else:
        body = listed_local
    return body(node_features, wq, wkv, wo, send_list, block_list, cotangent)


def solution(mesh):
    return jax.shard_map(
        local,
        mesh=mesh,
        in_specs=(
            P("graph", None, None),
            P(None, "mp", None),
            P(None, "mp", None),
            P("mp", None, None),
            P("graph", None, None),
            P("graph", None),
            P("graph", None),
        ),
        out_specs=(
            P(("graph", "mp"), None),
            P("graph", "mp", None),
            P("graph", "mp", None),
            P("mp", None, "graph"),
        ),
        check_vma=False,
    )
```
